32 devices in a mesh: gz: 16 (over z, x, core), ph: 2 (over y).
Axes of the slice: x: 2, y: 2, z: 4, core: 2. Of those that a mesh axis runs over, the one named last changes fastest.
Arguments:
- frac: bfloat16 [2, 128, 64, 256], P('ph', 'gz'), may hold values from 0.0099487305 to 0.099609375
- velocity: bfloat16 [2, 3, 128, 64, 256], P('ph', None, 'gz'), may hold values from -6 to 6
- gas_vel: bfloat16 [3, 128, 64, 256], P(None, 'gz'), may hold values from -6 to 6
- diameters: float32 [32], replicated, may hold values from 0.5 to 4
- phase_map: int32 [2], P('ph'), may hold values from 0 to 31
- wall_mask: int32 [64, 256], replicated, may hold values 0 or 1
- offsets: int32 [128], replicated, may hold values from 0 to 255
Outputs:
- pressure: float32 [128, 64, 256], P('gz')
- corrected: bfloat16 [2, 3, 128, 64, 256], P('ph', None, 'gz')
The draws below stay inside these ranges and needn't reach their ends.
Inputs may be any that keep to these rules, and one draw needn't show every extreme that they name: `wall_mask`: 1 marks a fluid cell, 0 a lifter or wall cell.
All inputs are finite; a program needn't handle non-finite values.
Results may differ from the reference program's by a relative error of at most 0.001.
Values sent between devices are 32-bit elements; how exact they have to be, the bound alone decides.
A program may use at most 64 MiB of HBM per device.

```python
import math
import jax
import jax.numpy as jnp
from jax import lax

NR = 64
NTH = 256
CLASSES = 32
NZ = 128
PHASES = 2


def draw_gas_vel(key, part):
    base = jax.random.normal(key, (3, NZ, NR, NTH), jnp.float32)
    return jnp.clip(base, -6.0, 6.0).astype(jnp.bfloat16)


def set_ends(result, stream_key, least, high):
    spot = [jax.random.randint(jax.random.fold_in(stream_key, axis), (), 0, length) for axis, length in enumerate(result.shape)]
    longest = result.shape.index(max(result.shape))
    beside = spot[:longest] + [(spot[longest] + 1) % result.shape[longest]] + spot[longest + 1:]
    return result.at[tuple(spot)].set(least).at[tuple(beside)].set(high)


def block_scale(key, shape, pieces, smallest, top_value):
    loudness, own = 1.0, jax.random.fold_in(key, 6)
    for dim, blocks in pieces:
        heights = jnp.exp(jax.random.uniform(jax.random.fold_in(own, dim), (blocks,), jnp.float32, smallest / len(pieces), top_value / len(pieces)))
        loudness = loudness * jnp.repeat(heights, shape[dim] // blocks).reshape([-1 if axis == dim else 1 for axis in range(len(shape))])
    return loudness


def bell_draw(own_key, dims, spread, limit, split=(), held_as=jnp.bfloat16):
    loudness = block_scale(own_key, dims, split, -0.22, 0.18) if split else 1.0
    result = jax.random.normal(own_key, dims, jnp.float32) * spread * loudness
    return jnp.minimum(jnp.maximum(result, -limit), limit).astype(held_as)


def setup_inputs(seed: int = 0) -> dict:
    arg_keys = jax.random.split(jax.random.key(seed), 8)
    return {
        "frac": jnp.clip(jnp.exp(math.log(0.099609375) - 2.3038113 * jax.random.uniform(arg_keys[0], (PHASES, NZ, NR, NTH), jnp.float32) ** block_scale(arg_keys[0], (PHASES, NZ, NR, NTH), ((0, 2), (1, 16)), -0.2, 0.2)), 0.0099487305, 0.099609375).astype(jnp.bfloat16),
        "velocity": bell_draw(arg_keys[1], (PHASES, 3, NZ, NR, NTH), 1.0, 6.0, ((0, 2), (2, 16))),
        "gas_vel": draw_gas_vel(jax.random.fold_in(arg_keys[7], 71), 0),
        "diameters": jnp.clip(jnp.exp(jax.random.uniform(arg_keys[3], (CLASSES,), jnp.float32, math.log(0.5), math.log(4.0))), 0.5, 4.0),
        "phase_map": jax.random.randint(arg_keys[4], (PHASES,), 0, CLASSES).astype(jnp.int32),
        "wall_mask": set_ends((jax.random.randint(arg_keys[5], (NR, NTH), 0, 4) < 3).astype(jnp.int32), jax.random.fold_in(arg_keys[5], 1), 0, 1),
        "offsets": set_ends(jax.random.randint(arg_keys[6], (NZ,), 0, NTH), jax.random.fold_in(arg_keys[6], 1), 0, NTH - 1).astype(jnp.int32),
    }


DT_STEP = 0.5
DRAG_SCALE = 20.0
COMPRESS = 0.005

def phase_terms(slot, frac, velocity, gas, diameters, phase_map):
    which = (jnp.arange(CLASSES, dtype=jnp.int32) == phase_map[slot]).astype(jnp.float32)
    size_here = jnp.sum(diameters * which)
    volume = frac[slot].astype(jnp.float32)
    slip = velocity[slot].astype(jnp.float32) - gas
    speed = jnp.sqrt(1.0 + lax.optimization_barrier(jnp.sum(slip * slip, 0)))
    beta = DRAG_SCALE * volume / (size_here * size_here) * (1.0 + 0.15 * speed)
    relax = 1.0 / (1.0 + DT_STEP * beta)
    return (volume, relax, slip)

def eigen_fft(count):
    wave = jnp.arange(count, dtype=jnp.float32)
    return 2.0 - 2.0 * jnp.cos(2.0 * math.pi / count * wave)

def reference(frac, velocity, gas_vel, diameters, phase_map, wall_mask, offsets):
    angle_step = 2.0 * math.pi / NTH
    around_idx = (jnp.arange(NTH, dtype=jnp.int32)[None, :] - offsets[:, None]) % NTH
    fluid = jnp.transpose(jnp.take(wall_mask, around_idx, axis=1), (1, 0, 2)).astype(jnp.float32)
    open_radial = fluid * jnp.concatenate([fluid[:, 1:], jnp.zeros_like(fluid[:, :1])], 1)
    open_around = fluid * jnp.roll(fluid, -1, 2)
    open_axial = fluid * jnp.roll(fluid, -1, 0)
    radii = (jnp.arange(NR, dtype=jnp.float32) + 0.5)[:, None]
    gas = gas_vel.astype(jnp.float32)
    total = gas
    for slot in range(PHASES):
        volume, relax, slip = phase_terms(slot, frac, velocity, gas, diameters, phase_map)
        total = total + volume * relax * slip
    flux_radial = total[0] * open_radial
    flux_around = total[1] * open_around
    flux_axial = total[2] * open_axial
    radial_prev = jnp.concatenate([jnp.zeros_like(flux_radial[:, :1]), flux_radial[:, :-1]], 1)
    source = ((radii + 0.5) * flux_radial - (radii - 0.5) * radial_prev) / radii
    source = source + (flux_around - jnp.roll(flux_around, 1, 2)) / (radii * angle_step)
    source = (source + flux_axial - jnp.roll(flux_axial, 1, 0)) / DT_STEP
    hat = jnp.fft.fft(jnp.fft.fft(source, axis=0), axis=2)
    stacked = jnp.stack([jnp.real(hat), jnp.imag(hat)], -1)
    right = -jnp.transpose(stacked, (0, 2, 1, 3))
    radius_vec = jnp.arange(NR, dtype=jnp.float32) + 0.5
    inner = radius_vec - 0.5
    outer = jnp.where(jnp.arange(NR) == NR - 1, 0.0, radius_vec + 0.5).astype(radius_vec.dtype)
    diag = COMPRESS + eigen_fft(NZ)[:, None, None] + eigen_fft(NTH)[None, :, None] / (radius_vec * angle_step) ** 2 + ((outer + inner) / radius_vec)[None, None, :]
    lower = jnp.broadcast_to(-inner / radius_vec, diag.shape)
    upper = jnp.broadcast_to(-outer / radius_vec, diag.shape)
    solved = jnp.stack([lax.linalg.tridiagonal_solve(lower, diag, upper, right[..., j:j + 1])[..., 0] for j in range(2)], -1)
    solved = jnp.transpose(solved, (0, 2, 1, 3))
    spectrum = lax.complex(solved[..., 0], solved[..., 1])
    pressure = jnp.real(jnp.fft.ifft(jnp.fft.ifft(spectrum, axis=0), axis=2)).astype(jnp.float32)
    radial_step = (jnp.concatenate([pressure[:, 1:], pressure[:, -1:]], 1) - pressure) * open_radial
    around_step = (jnp.roll(pressure, -1, 2) - pressure) / (radii * angle_step) * open_around
    axial_step = (jnp.roll(pressure, -1, 0) - pressure) * open_axial
    gradient = jnp.stack([radial_step, around_step, axial_step])
    results = []
    for slot in range(PHASES):
        volume, relax, slip = phase_terms(slot, frac, velocity, gas, diameters, phase_map)
        results.append((gas + relax * slip - DT_STEP * gradient).astype(jnp.bfloat16))
    return (pressure, jnp.stack(results))
```

```python
import functools
import math

import jax
import jax.numpy as jnp
import numpy as np
from jax import lax
from jax.experimental import pallas as pl
from jax.experimental.pallas import tpu as pltpu
from jax.sharding import PartitionSpec as P

DT_STEP = 0.5
DRAG_SCALE = 20.0
COMPRESS = 0.005
HIGHEST = lax.Precision.HIGHEST


def from_behind(block, axis, distance):
    devices = range(lax.axis_size(axis))
    route = [((i - distance) % len(devices), i) for i in devices]
    return lax.ppermute(block, axis, route)


def real_basis(count):
    index_rows = jnp.arange(count, dtype=jnp.int32)[:, None]
    column = jnp.arange(count, dtype=jnp.int32)[None, :]
    half = count // 2
    wave = jnp.where(column <= half, column, column - half)
    angle = 2.0 * math.pi / count * (index_rows * wave % count).astype(jnp.float32)
    scaled = math.sqrt(2.0 / count)
    cosine = jnp.cos(angle)
    table = jnp.where(column < half, scaled * cosine, scaled * jnp.sin(angle))
    return jnp.where((column == 0) | (column == half), cosine / math.sqrt(count), table)


def eigen_values(count):
    column = jnp.arange(count, dtype=jnp.int32)
    half = count // 2
    wave = jnp.where(column <= half, column, column - half).astype(jnp.float32)
    return 2.0 - 2.0 * jnp.cos(2.0 * math.pi / count * wave)


def rotate_mask(wall_mask, turns, around_count):
    around_idx = (
        jnp.arange(around_count, dtype=jnp.int32)[None, :] - turns[:, None]
    ) % around_count
    return jnp.transpose(jnp.take(wall_mask, around_idx, axis=1), (1, 0, 2)).astype(jnp.float32)


def radial_solve(spectral, axial_eig, theta_eig, radius_vec, angle_step):
    radial_count = radius_vec.shape[0]
    inner = radius_vec - 0.5
    outer = jnp.where(jnp.arange(radial_count) == radial_count - 1, 0.0, radius_vec + 0.5)
    diag = (
        COMPRESS
        + axial_eig[:, None, None]
        + theta_eig[None, :, None] / (radius_vec * angle_step) ** 2
        + ((outer + inner) / radius_vec)[None, None, :]
    )
    lower = jnp.broadcast_to(-inner / radius_vec, diag.shape)
    upper = jnp.broadcast_to(-outer / radius_vec, diag.shape)
    right = -jnp.transpose(spectral, (0, 2, 1))[..., None]
    solved = lax.linalg.tridiagonal_solve(lower, diag, upper, right)[..., 0]
    return jnp.transpose(solved, (0, 2, 1))


def to_space(modes, around_table):
    return jnp.dot(
        modes.reshape(-1, around_table.shape[0]), around_table.T, precision=HIGHEST
    ).reshape(modes.shape)


def shards(frac, velocity, gas_vel, diameters, phase_map, wall_mask, offsets):
    plane_count = frac.shape[1]
    radial_count = frac.shape[2]
    around_count = frac.shape[3]
    axial_total = offsets.shape[0]
    phase_count = lax.axis_size("ph")
    slab_index = lax.axis_index("gz")
    first_plane = slab_index * plane_count
    angle_step = 2.0 * math.pi / around_count
    plane_ids = (first_plane + jnp.arange(plane_count + 1, dtype=jnp.int32)) % axial_total
    fluid_all = rotate_mask(wall_mask, jnp.take(offsets, plane_ids), around_count)
    fluid = fluid_all[:plane_count]
    open_radial = fluid * jnp.concatenate([fluid[:, 1:], jnp.zeros_like(fluid[:, :1])], 1)
    open_around = fluid * jnp.roll(fluid, -1, 2)
    open_axial = fluid * fluid_all[1:]
    radius_vec = jnp.arange(radial_count, dtype=jnp.float32) + 0.5
    radii = radius_vec[:, None]
    which = (jnp.arange(diameters.shape[0], dtype=jnp.int32) == phase_map[0]).astype(jnp.float32)
    size_here = jnp.sum(diameters * which)
    volume = frac[0].astype(jnp.float32)
    gas = gas_vel.astype(jnp.float32)
    slip = velocity[0].astype(jnp.float32) - gas
    speed = jnp.sqrt(1.0 + jnp.sum(slip * slip, 0))
    beta = DRAG_SCALE * volume / (size_here * size_here) * (1.0 + 0.15 * speed)
    relax = 1.0 / (1.0 + DT_STEP * beta)
    predicted = gas + relax * slip
    share = volume * relax * slip + gas / phase_count
    flux_radial = share[0] * open_radial
    flux_around = share[1] * open_around
    flux_axial = share[2] * open_axial
    below = from_behind(flux_axial[-1:], "gz", 1)
    axial_prev = jnp.concatenate([below, flux_axial[:-1]], 0)
    radial_prev = jnp.concatenate([jnp.zeros_like(flux_radial[:, :1]), flux_radial[:, :-1]], 1)
    term = ((radii + 0.5) * flux_radial - (radii - 0.5) * radial_prev) / radii
    term = term + (flux_around - jnp.roll(flux_around, 1, 2)) / (radii * angle_step)
    term = (term + flux_axial - axial_prev) / DT_STEP
    around_table = real_basis(around_count)
    axial_table = real_basis(axial_total)
    axial_eig = eigen_values(axial_total)
    axial_step = None
    source = lax.psum(term, "ph")
    modes = jnp.dot(source.reshape(-1, around_count), around_table, precision=HIGHEST).reshape(
        source.shape
    )
    pencil = lax.all_to_all(modes, "gz", split_axis=2, concat_axis=0, tiled=True)
    mode_count = pencil.shape[2]
    theta_eig = lax.dynamic_slice_in_dim(
        eigen_values(around_count), slab_index * mode_count, mode_count
    )
    flat = pencil.reshape(axial_total, -1)
    spectral = jnp.dot(axial_table.T, flat, precision=HIGHEST).reshape(pencil.shape)
    solved = radial_solve(spectral, axial_eig, theta_eig, radius_vec, angle_step)
    space = jnp.dot(axial_table, solved.reshape(axial_total, -1), precision=HIGHEST).reshape(
        pencil.shape
    )
    ahead = jnp.roll(space, -1, 0) - space
    back, back_step = (
        lax.all_to_all(space, "gz", split_axis=0, concat_axis=2, tiled=True),
        lax.all_to_all(ahead, "gz", split_axis=0, concat_axis=2, tiled=True),
    )
    pressure = to_space(back, around_table)
    axial_step = to_space(back_step, around_table)
    radial_step = (jnp.concatenate([pressure[:, 1:], pressure[:, -1:]], 1) - pressure) * open_radial
    around_step = (jnp.roll(pressure, -1, 2) - pressure) / (radii * angle_step) * open_around
    gradient = jnp.stack([radial_step, around_step, axial_step * open_axial])
    corrected = (predicted - DT_STEP * gradient).astype(jnp.bfloat16)[None]
    return (pressure, corrected)


MESH_ID = pl.DeviceIdType.MESH


def split_low(x):
    high = x.astype(jnp.bfloat16)
    return high, (x - high.astype(jnp.float32)).astype(jnp.bfloat16)


def triple_dot(x, table_high, table_low):
    high, low = split_low(x)
    out = jnp.dot(high, table_high, preferred_element_type=jnp.float32)
    out = out + jnp.dot(low, table_high, preferred_element_type=jnp.float32)
    return out + jnp.dot(high, table_low, preferred_element_type=jnp.float32)


def np_high_low(table):
    high = table.astype(jnp.bfloat16)
    low = (table - high.astype(np.float64)).astype(jnp.bfloat16)
    return high, low


@functools.lru_cache(maxsize=None)
def operator_tables(radial, around, axial, planes):
    half = around // 2
    rows = np.arange(around)[:, None]
    column = np.arange(around)[None, :]
    wave = np.where(column <= half, column, column - half)
    angle = 2.0 * np.pi / around * (rows * wave % around)
    basis = np.sqrt(2.0 / around) * np.where(column <= half, np.cos(angle), np.sin(angle))
    basis = np.where((column == 0) | (column == half), np.cos(angle) / np.sqrt(around), basis)
    radius = np.arange(radial) + 0.5
    inner = radius - 0.5
    outer = np.where(np.arange(radial) == radial - 1, 0.0, radius + 0.5)
    step = 2.0 * np.pi / around
    vectors, values = [], []
    for m in range(half + 1):
        eig = 2.0 - 2.0 * np.cos(2.0 * np.pi / around * m)
        matrix = np.diag((outer + inner) / radius + eig / (radius * step) ** 2)
        off = -outer[:-1] / np.sqrt(radius[:-1] * radius[1:])
        matrix = matrix + np.diag(off, 1) + np.diag(off, -1)
        value, vector = np.linalg.eigh(matrix)
        vector = vector * np.where(vector[:1] < 0.0, -1.0, 1.0)
        values.append(value)
        vectors.append(vector)
    vectors = np.stack(vectors, -1)
    values = np.maximum(np.stack(values, -1), 0.0)
    first = vectors[:, :, :half]
    nyquist = np.zeros((radial, max(radial, 128)))
    nyquist[:, :radial] = vectors[:, :, half].T
    other = np.concatenate([values[:, half:], values[:, 1:half]], -1)
    over = COMPRESS + np.stack([values[:, :half], other])
    root = np.sqrt(over * (over + 4.0))
    ratio = 2.0 / (2.0 + over + root)
    jump = ratio**planes
    wrap = 1.0 / (1.0 - ratio**axial)
    line = np.stack([ratio, 1.0 / root, jump, wrap], 1).astype(np.float32)
    ahead = np_high_low(basis)
    back = np_high_low(basis.T.copy())
    return (
        first.astype(np.float32),
        nyquist.astype(np.float32),
        line,
        np.stack(ahead),
        np.stack(back),
    )


def drum_kernel(
    gz_count,
    offsets_ref,
    diameters_ref,
    map_ref,
    wall_hbm,
    frac_hbm,
    velocity_hbm,
    gas_hbm,
    ahead_hbm,
    nyquist_hbm,
    line_hbm,
    back_hbm,
    radial_hbm,
    pressure_ref,
    corrected_ref,
    wall_ref,
    frac_ref,
    velocity_ref,
    gas_ref,
    ahead_ref,
    nyquist_ref,
    line_ref,
    back_ref,
    fluid,
    pred,
    term,
    axial_flux,
    halo,
    modes,
    partner,
    radial,
    radial_back,
    lines,
    ends_out,
    ends_in,
    states_out,
    states_in,
    solved,
    result,
    table_sem,
    input_sem,
    halo_sem,
    swap_send,
    swap_recv,
    ends_send,
    ends_recv,
    states_send,
    states_recv,
    back_send,
    back_recv,
):
    me = lax.axis_index("gz")
    ph = lax.axis_index("ph")
    other = 1 - ph
    planes, rows, around = term.shape
    half = around // 2
    axial_total = offsets_ref.shape[0]
    blocks = rows // 8
    angle_step = 2.0 * math.pi / around

    barrier = pltpu.get_barrier_semaphore()
    for hop in range(1, gz_count):
        pl.semaphore_signal(
            barrier, inc=1, device_id=(lax.rem(me + hop, gz_count), ph), device_id_type=MESH_ID
        )
    pl.semaphore_signal(barrier, inc=1, device_id=(me, other), device_id_type=MESH_ID)

    pairs = (
        (wall_hbm, wall_ref),
        (frac_hbm, frac_ref),
        (velocity_hbm, velocity_ref),
        (gas_hbm, gas_ref),
        (ahead_hbm, ahead_ref),
        (nyquist_hbm, nyquist_ref),
        (line_hbm, line_ref),
        (back_hbm, back_ref),
    )
    fetches = [pltpu.make_async_copy(a, b, input_sem.at[i]) for i, (a, b) in enumerate(pairs)]
    table_copy = pltpu.make_async_copy(radial_hbm, radial, table_sem)
    for fetch in fetches[:5]:
        fetch.start()
    table_copy.start()
    for fetch in fetches[5:]:
        fetch.start()
    fetches[0].wait()

    radii = lax.broadcasted_iota(jnp.int32, (rows, around), 0).astype(jnp.float32) + 0.5
    row_id = lax.broadcasted_iota(jnp.int32, (rows, around), 0)
    wall = wall_ref[...].astype(jnp.float32).astype(jnp.bfloat16)
    from_col = lax.broadcasted_iota(jnp.int32, (around, around), 0)
    to_col = lax.broadcasted_iota(jnp.int32, (around, around), 1)
    gap = to_col - from_col

    def rotate(z, carry):
        turn = offsets_ref[lax.rem(me * planes + z, axial_total)]
        hit = (gap == turn) | (gap == turn - around)
        one_hot = jnp.where(hit, 1.0, 0.0).astype(jnp.bfloat16)
        fluid[z] = jnp.dot(wall, one_hot, preferred_element_type=jnp.float32)
        return carry

    lax.fori_loop(0, planes + 1, rotate, 0)

    for fetch in fetches[1:4]:
        fetch.wait()
    size = diameters_ref[map_ref[0]]
    axial_flux[0] = jnp.zeros((rows, around), jnp.float32)

    def opens(z):
        here = fluid[z]
        open_radial = jnp.where(row_id == rows - 1, 0.0, here * pltpu.roll(here, rows - 1, 0))
        open_around = here * pltpu.roll(here, around - 1, 1)
        return open_radial, open_around, here * fluid[z + 1]

    weight = -jnp.sqrt(radii) / DT_STEP
    share = 1.0 / lax.axis_size("ph")

    def source(z, carry):
        volume = frac_ref[0, z].astype(jnp.float32)
        gas = [gas_ref[a, z].astype(jnp.float32) for a in range(3)]
        slip = [velocity_ref[0, a, z].astype(jnp.float32) - gas[a] for a in range(3)]
        speed = jnp.sqrt(1.0 + (slip[0] * slip[0] + slip[1] * slip[1] + slip[2] * slip[2]))
        beta = DRAG_SCALE * volume / (size * size) * (1.0 + 0.15 * speed)
        relax = 1.0 / (1.0 + DT_STEP * beta)
        open_radial, open_around, open_axial = opens(z)
        for a in range(3):
            pred[a, z] = gas[a] + relax * slip[a]
        pull = volume * relax
        flux_radial = (pull * slip[0] + share * gas[0]) * open_radial
        flux_around = (pull * slip[1] + share * gas[1]) * open_around
        flux_axial = (pull * slip[2] + share * gas[2]) * open_axial
        axial_flux[z + 1] = flux_axial
        out = (radii + 0.5) * flux_radial
        inward = jnp.where(row_id == 0, 0.0, pltpu.roll(out, 1, 0))
        total = (out - inward) / radii
        total = total + (flux_around - pltpu.roll(flux_around, 1, 1)) / (radii * angle_step)
        term[z] = (total + flux_axial - axial_flux[z]) * weight
        return carry

    lax.fori_loop(0, planes, source, 0)

    fetches[4].wait()
    pl.semaphore_wait(barrier, gz_count)

    halo_copy = pltpu.make_async_remote_copy(
        src_ref=axial_flux.at[planes],
        dst_ref=halo,
        send_sem=halo_sem.at[0],
        recv_sem=halo_sem.at[1],
        device_id=(lax.rem(me + 1, gz_count), ph),
        device_id_type=MESH_ID,
    )
    halo_copy.start()

    def swap(z):
        return pltpu.make_async_remote_copy(
            src_ref=modes.at[other, z],
            dst_ref=partner.at[z],
            send_sem=swap_send.at[z],
            recv_sem=swap_recv.at[z],
            device_id=(me, other),
            device_id_type=MESH_ID,
        )

    def to_modes(z, value):
        out = triple_dot(value, ahead_ref[0], ahead_ref[1])
        modes[0, z] = out[:, :half]
        modes[1, z] = out[:, half:]
        swap(z).start()

    def send_modes(k, carry):
        to_modes(k, term[k])
        return carry

    lax.fori_loop(1, planes, send_modes, 0)
    halo_copy.wait()
    to_modes(0, term[0] - halo[...] * weight)

    table_copy.wait()
    for fetch in fetches[5:]:
        fetch.wait()
    is_other = jnp.where(ph == 1, 1, 0)
    lane0 = (lax.broadcasted_iota(jnp.int32, (rows, half), 1) == 0) & (
        jnp.broadcast_to(is_other, (rows, half)) == 1
    )
    for r in range(rows):
        fill = jnp.broadcast_to(nyquist_ref[:, r : r + 1], (rows, half))
        radial[pl.ds(r * rows, rows), :] = jnp.where(lane0, fill, radial[pl.ds(r * rows, rows), :])

    def apply(table, load, z):
        def add(k, acc):
            for j in range(8):
                r = k * 8 + j
                line = jnp.broadcast_to(load(z, r), (rows, half))
                acc = acc + table[pl.ds(pl.multiple_of(r * rows, rows), rows), :] * line
            return acc

        return lax.fori_loop(0, rows // 8, add, jnp.zeros((rows, half), jnp.float32))

    def load_term(z, r):
        return modes[ph, z, pl.ds(r, 1), :] + partner[z, pl.ds(r, 1), :]

    def forward(k, carry):
        z = lax.rem(k + 1, planes)
        swap(z).wait_recv()
        lines[z] = apply(radial, load_term, z)
        return carry

    lax.fori_loop(0, planes, forward, 0)

    ratio = line_ref[ph, 0]
    rising = lines[0]
    for z in range(1, planes):
        rising = rising * ratio + lines[z]
    falling = lines[planes - 1]
    for z in range(planes - 2, -1, -1):
        falling = falling * ratio + lines[z]
    for j in range(blocks):
        ends_out[j] = rising[8 * j : 8 * j + 8]
        ends_out[blocks + j] = falling[8 * j : 8 * j + 8]

    def exchange(src, dst, send, recv, hop, sender):
        to = lax.rem(me + hop, gz_count)
        at = lax.rem(me + gz_count - hop, gz_count) if sender else me
        return pltpu.make_async_remote_copy(
            src_ref=src.at[to],
            dst_ref=dst.at[at],
            send_sem=send.at[hop],
            recv_sem=recv.at[hop],
            device_id=(to, ph),
            device_id_type=MESH_ID,
        )

    for hop in range(1, gz_count):
        exchange(ends_out, ends_in, ends_send, ends_recv, hop, False).start()
    ends_in[me] = ends_out[me]

    def flip(l, carry):
        radial_back[pl.ds(pl.multiple_of(l * rows, rows), rows), :] = radial[
            pl.ds(l, rows, stride=rows), :
        ]
        return carry

    lax.fori_loop(0, rows, flip, 0)

    for hop in range(1, gz_count):
        exchange(ends_out, ends_in, ends_send, ends_recv, hop, True).wait_recv()

    is_rise = 1 - me // blocks
    mine = lax.rem(me, blocks)
    jump = line_ref[ph, 2, pl.ds(pl.multiple_of(mine * 8, 8), 8), :]
    wrap = line_ref[ph, 3, pl.ds(pl.multiple_of(mine * 8, 8), 8), :]
    order = [is_rise * s + (1 - is_rise) * (gz_count - 1 - s) for s in range(gz_count)]
    state = jnp.zeros((8, half), jnp.float32)
    for s in range(gz_count):
        state = state * jump + ends_in[order[s]]
    state = state * wrap
    for s in range(gz_count):
        states_out[order[s]] = state
        state = state * jump + ends_in[order[s]]

    for hop in range(1, gz_count):
        exchange(states_out, states_in, states_send, states_recv, hop, False).start()
    states_in[me] = states_out[me]
    for hop in range(1, gz_count):
        exchange(states_out, states_in, states_send, states_recv, hop, True).wait_recv()

    scale = line_ref[ph, 1]
    right = jnp.concatenate([states_in[blocks + j] for j in range(blocks)], 0)
    left = jnp.concatenate([states_in[j] for j in range(blocks)], 0)
    solved[planes] = right
    behind = right * ratio
    for z in range(planes - 1, -1, -1):
        solved[z] = behind
        behind = (behind + lines[z]) * ratio
    ahead_state = left
    for z in range(planes):
        ahead_state = ahead_state * ratio + lines[z]
        solved[z] = (solved[z] + ahead_state) * scale
    solved[planes] = (solved[planes] + ahead_state * ratio) * scale

    def give(z, index):
        return pltpu.make_async_remote_copy(
            src_ref=result.at[index, z],
            dst_ref=result.at[index, z],
            send_sem=back_send.at[z],
            recv_sem=back_recv.at[z],
            device_id=(me, other),
            device_id_type=MESH_ID,
        )

    def load_solved(z, r):
        return solved[z, pl.ds(r, 1), :]

    shrink = 1.0 / jnp.sqrt(radii[:, :half])

    def inverse(z, carry):
        result[ph, z] = apply(radial_back, load_solved, z) * shrink
        give(z, ph).start()
        return carry

    lax.fori_loop(0, planes + 1, inverse, 0)

    arc = 1.0 / (radii * angle_step)

    def finish(z):
        give(z, other).wait_recv()
        both = jnp.concatenate([result[0, z], result[1, z]], 1)
        return triple_dot(both, back_ref[0], back_ref[1])

    def correct(z, here):
        later = finish(z + 1)
        pressure_ref[z] = here
        open_radial, open_around, open_axial = opens(z)
        radial_step = (pltpu.roll(here, rows - 1, 0) - here) * open_radial
        around_step = (pltpu.roll(here, around - 1, 1) - here) * arc * open_around
        axial_step = (later - here) * open_axial
        for a, step in enumerate((radial_step, around_step, axial_step)):
            corrected_ref[0, a, z] = (pred[a, z] - DT_STEP * step).astype(jnp.bfloat16)
        return later

    lax.fori_loop(0, planes, correct, finish(0))

    for z in range(planes):
        swap(z).wait_send()
    for hop in range(1, gz_count):
        exchange(ends_out, ends_in, ends_send, ends_recv, hop, False).wait_send()
        exchange(states_out, states_in, states_send, states_recv, hop, False).wait_send()
    for z in range(planes + 1):
        give(z, ph).wait_send()


def drum_step(gz_count, frac, velocity, gas_vel, diameters, phase_map, wall_mask, offsets):
    planes, rows, around = frac.shape[1:]
    half = around // 2
    first, nyquist, line, ahead, back = operator_tables(rows, around, offsets.shape[0], planes)
    smem = pl.BlockSpec(memory_space=pltpu.SMEM)
    f32 = jnp.float32
    dma = pltpu.SemaphoreType.DMA
    ends = (gz_count, 8, half)
    return pl.pallas_call(
        functools.partial(drum_kernel, gz_count),
        out_shape=(
            pltpu.VMEM((planes, rows, around), f32),
            pltpu.VMEM((1, 3, planes, rows, around), jnp.bfloat16),
        ),
        in_specs=[smem] * 3 + [pl.BlockSpec(memory_space=pl.ANY)] * 9,
        out_specs=[pl.BlockSpec(memory_space=pltpu.VMEM)] * 2,
        scratch_shapes=[
            pltpu.VMEM(wall_mask.shape, jnp.int32),
            pltpu.VMEM(frac.shape, jnp.bfloat16),
            pltpu.VMEM(velocity.shape, jnp.bfloat16),
            pltpu.VMEM(gas_vel.shape, jnp.bfloat16),
            pltpu.VMEM(ahead.shape, jnp.bfloat16),
            pltpu.VMEM(nyquist.shape, f32),
            pltpu.VMEM(line.shape, f32),
            pltpu.VMEM(back.shape, jnp.bfloat16),
            pltpu.VMEM((planes + 1, rows, around), f32),
            pltpu.VMEM((3, planes, rows, around), f32),
            pltpu.VMEM((planes, rows, around), f32),
            pltpu.VMEM((planes + 1, rows, around), f32),
            pltpu.VMEM((rows, around), f32),
            pltpu.VMEM((2, planes, rows, half), f32),
            pltpu.VMEM((planes, rows, half), f32),
            pltpu.VMEM((rows * rows, half), f32),
            pltpu.VMEM((rows * rows, half), f32),
            pltpu.VMEM((planes, rows, half), f32),
            pltpu.VMEM(ends, f32),
            pltpu.VMEM(ends, f32),
            pltpu.VMEM(ends, f32),
            pltpu.VMEM(ends, f32),
            pltpu.VMEM((planes + 1, rows, half), f32),
            pltpu.VMEM((2, planes + 1, rows, half), f32),
            dma,
            dma((8,)),
            dma((2,)),
            dma((planes,)),
            dma((planes,)),
            dma((gz_count,)),
            dma((gz_count,)),
            dma((gz_count,)),
            dma((gz_count,)),
            dma((planes + 1,)),
            dma((planes + 1,)),
        ],
        compiler_params=pltpu.CompilerParams(
            collective_id=0, has_side_effects=True, vmem_limit_bytes=56 * 1024 * 1024
        ),
    )(
        offsets,
        diameters,
        phase_map,
        wall_mask,
        frac,
        velocity,
        gas_vel,
        jnp.asarray(ahead),
        jnp.asarray(nyquist),
        jnp.asarray(line),
        jnp.asarray(back),
        jnp.asarray(first.reshape(rows * rows, half)),
    )


def solution(mesh):
    in_specs = (
        P("ph", "gz", None, None),
        P("ph", None, "gz", None, None),
        P(None, "gz", None, None),
        P(),
        P("ph"),
        P(),
        P(),
    )
    out_specs = (P("gz", None, None), P("ph", None, "gz", None, None))
    gz_count, ph_count = mesh.shape["gz"], mesh.shape["ph"]

    def body(frac, *rest):
        rows, around = frac.shape[2:]
        fits = ph_count == 2 and around == 256 and rows <= 128
        if fits and rows * 2 == gz_count * 8 and frac.shape[1] <= 8:
            return drum_step(gz_count, frac, *rest)
        return shards(frac, *rest)

    return jax.shard_map(body, mesh=mesh, in_specs=in_specs, out_specs=out_specs, check_vma=False)
```

```python
import functools
import math

import jax
import jax.numpy as jnp
import numpy as np
from jax import lax
from jax.experimental import pallas as pl
from jax.experimental.pallas import tpu as pltpu
from jax.sharding import PartitionSpec as P

DT_STEP = 0.5
DRAG_SCALE = 20.0
COMPRESS = 0.005
HIGHEST = lax.Precision.HIGHEST


def from_behind(block, axis, distance):
    devices = range(lax.axis_size(axis))
    route = [((i - distance) % len(devices), i) for i in devices]
    return lax.ppermute(block, axis, route)


def real_basis(count):
    index_rows = jnp.arange(count, dtype=jnp.int32)[:, None]
    column = jnp.arange(count, dtype=jnp.int32)[None, :]
    half = count // 2
    wave = jnp.where(column <= half, column, column - half)
    angle = 2.0 * math.pi / count * (index_rows * wave % count).astype(jnp.float32)
    scaled = math.sqrt(2.0 / count)
    cosine = jnp.cos(angle)
    table = jnp.where(column < half, scaled * cosine, scaled * jnp.sin(angle))
    return jnp.where((column == 0) | (column == half), cosine / math.sqrt(count), table)


def eigen_values(count):
    column = jnp.arange(count, dtype=jnp.int32)
    half = count // 2
    wave = jnp.where(column <= half, column, column - half).astype(jnp.float32)
    return 2.0 - 2.0 * jnp.cos(2.0 * math.pi / count * wave)


def rotate_mask(wall_mask, turns, around_count):
    around_idx = (
        jnp.arange(around_count, dtype=jnp.int32)[None, :] - turns[:, None]
    ) % around_count
    return jnp.transpose(jnp.take(wall_mask, around_idx, axis=1), (1, 0, 2)).astype(jnp.float32)


def radial_solve(spectral, axial_eig, theta_eig, radius_vec, angle_step):
    radial_count = radius_vec.shape[0]
    inner = radius_vec - 0.5
    outer = jnp.where(jnp.arange(radial_count) == radial_count - 1, 0.0, radius_vec + 0.5)
    diag = (
        COMPRESS
        + axial_eig[:, None, None]
        + theta_eig[None, :, None] / (radius_vec * angle_step) ** 2
        + ((outer + inner) / radius_vec)[None, None, :]
    )
    lower = jnp.broadcast_to(-inner / radius_vec, diag.shape)
    upper = jnp.broadcast_to(-outer / radius_vec, diag.shape)
    right = -jnp.transpose(spectral, (0, 2, 1))[..., None]
    solved = lax.linalg.tridiagonal_solve(lower, diag, upper, right)[..., 0]
    return jnp.transpose(solved, (0, 2, 1))


def to_space(modes, around_table):
    return jnp.dot(
        modes.reshape(-1, around_table.shape[0]), around_table.T, precision=HIGHEST
    ).reshape(modes.shape)


def shards(frac, velocity, gas_vel, diameters, phase_map, wall_mask, offsets):
    plane_count = frac.shape[1]
    radial_count = frac.shape[2]
    around_count = frac.shape[3]
    axial_total = offsets.shape[0]
    phase_count = lax.axis_size("ph")
    slab_index = lax.axis_index("gz")
    first_plane = slab_index * plane_count
    angle_step = 2.0 * math.pi / around_count
    plane_ids = (first_plane + jnp.arange(plane_count + 1, dtype=jnp.int32)) % axial_total
    fluid_all = rotate_mask(wall_mask, jnp.take(offsets, plane_ids), around_count)
    fluid = fluid_all[:plane_count]
    open_radial = fluid * jnp.concatenate([fluid[:, 1:], jnp.zeros_like(fluid[:, :1])], 1)
    open_around = fluid * jnp.roll(fluid, -1, 2)
    open_axial = fluid * fluid_all[1:]
    radius_vec = jnp.arange(radial_count, dtype=jnp.float32) + 0.5
    radii = radius_vec[:, None]
    which = (jnp.arange(diameters.shape[0], dtype=jnp.int32) == phase_map[0]).astype(jnp.float32)
    size_here = jnp.sum(diameters * which)
    volume = frac[0].astype(jnp.float32)
    gas = gas_vel.astype(jnp.float32)
    slip = velocity[0].astype(jnp.float32) - gas
    speed = jnp.sqrt(1.0 + jnp.sum(slip * slip, 0))
    beta = DRAG_SCALE * volume / (size_here * size_here) * (1.0 + 0.15 * speed)
    relax = 1.0 / (1.0 + DT_STEP * beta)
    predicted = gas + relax * slip
    share = volume * relax * slip + gas / phase_count
    flux_radial = share[0] * open_radial
    flux_around = share[1] * open_around
    flux_axial = share[2] * open_axial
    below = from_behind(flux_axial[-1:], "gz", 1)
    axial_prev = jnp.concatenate([below, flux_axial[:-1]], 0)
    radial_prev = jnp.concatenate([jnp.zeros_like(flux_radial[:, :1]), flux_radial[:, :-1]], 1)
    term = ((radii + 0.5) * flux_radial - (radii - 0.5) * radial_prev) / radii
    term = term + (flux_around - jnp.roll(flux_around, 1, 2)) / (radii * angle_step)
    term = (term + flux_axial - axial_prev) / DT_STEP
    around_table = real_basis(around_count)
    axial_table = real_basis(axial_total)
    axial_eig = eigen_values(axial_total)
    axial_step = None
    source = lax.psum(term, "ph")
    modes = jnp.dot(source.reshape(-1, around_count), around_table, precision=HIGHEST).reshape(
        source.shape
    )
    pencil = lax.all_to_all(modes, "gz", split_axis=2, concat_axis=0, tiled=True)
    mode_count = pencil.shape[2]
    theta_eig = lax.dynamic_slice_in_dim(
        eigen_values(around_count), slab_index * mode_count, mode_count
    )
    flat = pencil.reshape(axial_total, -1)
    spectral = jnp.dot(axial_table.T, flat, precision=HIGHEST).reshape(pencil.shape)
    solved = radial_solve(spectral, axial_eig, theta_eig, radius_vec, angle_step)
    space = jnp.dot(axial_table, solved.reshape(axial_total, -1), precision=HIGHEST).reshape(
        pencil.shape
    )
    ahead = jnp.roll(space, -1, 0) - space
    back, back_step = (
        lax.all_to_all(space, "gz", split_axis=0, concat_axis=2, tiled=True),
        lax.all_to_all(ahead, "gz", split_axis=0, concat_axis=2, tiled=True),
    )
    pressure = to_space(back, around_table)
    axial_step = to_space(back_step, around_table)
    radial_step = (jnp.concatenate([pressure[:, 1:], pressure[:, -1:]], 1) - pressure) * open_radial
    around_step = (jnp.roll(pressure, -1, 2) - pressure) / (radii * angle_step) * open_around
    gradient = jnp.stack([radial_step, around_step, axial_step * open_axial])
    corrected = (predicted - DT_STEP * gradient).astype(jnp.bfloat16)[None]
    return (pressure, corrected)


MESH_ID = pl.DeviceIdType.MESH


def split_low(x):
    high = x.astype(jnp.bfloat16)
    return high, (x - high.astype(jnp.float32)).astype(jnp.bfloat16)


def triple_dot(x, table_high, table_low):
    high, low = split_low(x)
    out = jnp.dot(high, table_high, preferred_element_type=jnp.float32)
    out = out + jnp.dot(low, table_high, preferred_element_type=jnp.float32)
    return out + jnp.dot(high, table_low, preferred_element_type=jnp.float32)


def np_high_low(table):
    high = table.astype(jnp.bfloat16)
    low = (table - high.astype(np.float64)).astype(jnp.bfloat16)
    return high, low


@functools.lru_cache(maxsize=None)
def operator_tables(radial, around, axial, planes):
    half = around // 2
    rows = np.arange(around)[:, None]
    column = np.arange(around)[None, :]
    wave = np.where(column <= half, column, column - half)
    angle = 2.0 * np.pi / around * (rows * wave % around)
    basis = np.sqrt(2.0 / around) * np.where(column <= half, np.cos(angle), np.sin(angle))
    basis = np.where((column == 0) | (column == half), np.cos(angle) / np.sqrt(around), basis)
    radius = np.arange(radial) + 0.5
    inner = radius - 0.5
    outer = np.where(np.arange(radial) == radial - 1, 0.0, radius + 0.5)
    step = 2.0 * np.pi / around
    vectors, values = [], []
    for m in range(half + 1):
        eig = 2.0 - 2.0 * np.cos(2.0 * np.pi / around * m)
        matrix = np.diag((outer + inner) / radius + eig / (radius * step) ** 2)
        off = -outer[:-1] / np.sqrt(radius[:-1] * radius[1:])
        matrix = matrix + np.diag(off, 1) + np.diag(off, -1)
        value, vector = np.linalg.eigh(matrix)
        vector = vector * np.where(vector[:1] < 0.0, -1.0, 1.0)
        values.append(value)
        vectors.append(vector)
    vectors = np.stack(vectors, -1)
    values = np.maximum(np.stack(values, -1), 0.0)
    first = vectors[:, :, :half]
    last = vectors[:, :, half]
    other = np.concatenate([values[:, half:], values[:, 1:half]], -1)
    over = COMPRESS + np.stack([values[:, :half], other])
    root = np.sqrt(over * (over + 4.0))
    ratio = 2.0 / (2.0 + over + root)
    jump = ratio**planes
    wrap = 1.0 / (1.0 - ratio**axial)
    line = np.stack([ratio, 1.0 / root, jump, wrap], 1).astype(np.float32)
    ahead = np_high_low(basis)
    back = np_high_low(basis.T.reshape(2, half, around))
    nyquist = np_high_low(np.stack([last.T, last]))
    return (
        first.astype(np.float32),
        np.stack(nyquist),
        line,
        np.stack(ahead),
        np.stack(back),
    )


def left_triple(table_high, table_low, x):
    high, low = split_low(x)
    out = jnp.dot(table_high, high, preferred_element_type=jnp.float32)
    out = out + jnp.dot(table_high, low, preferred_element_type=jnp.float32)
    return out + jnp.dot(table_low, high, preferred_element_type=jnp.float32)


def drum_kernel(
    gz_count,
    group,
    offsets_ref,
    diameters_ref,
    map_ref,
    wall_hbm,
    frac_hbm,
    velocity_hbm,
    gas_hbm,
    ahead_hbm,
    nyquist_hbm,
    line_hbm,
    back_hbm,
    radial_hbm,
    pressure_ref,
    corrected_ref,
    wall_ref,
    frac_ref,
    velocity_ref,
    gas_ref,
    ahead_ref,
    nyquist_ref,
    line_ref,
    back_ref,
    radial,
    radial_back,
    fluid,
    pred,
    term,
    axial_flux,
    halo,
    modes,
    partner,
    lines,
    ends_out,
    ends_in,
    states_out,
    states_in,
    solved,
    space,
    input_sem,
    halo_sem,
    swap_send,
    swap_recv,
    lines_sem,
    ends_sem,
    states_send,
    states_recv,
    relay_sem,
):
    me = lax.axis_index("gz")
    ph = lax.axis_index("ph")
    other = 1 - ph
    planes, rows, around = term.shape
    half = around // 2
    axial_total = offsets_ref.shape[0]
    blocks = rows // 8
    angle_step = 2.0 * math.pi / around

    pairs = (
        (wall_hbm, wall_ref),
        (frac_hbm, frac_ref),
        (velocity_hbm, velocity_ref),
        (gas_hbm, gas_ref),
        (ahead_hbm, ahead_ref),
        (radial_hbm, radial),
        (nyquist_hbm, nyquist_ref),
        (line_hbm, line_ref),
        (back_hbm, back_ref),
    )
    fetches = [pltpu.make_async_copy(a, b, input_sem.at[i]) for i, (a, b) in enumerate(pairs)]
    for fetch in fetches[:4]:
        fetch.start()
    barrier = pltpu.get_barrier_semaphore()
    for hop in range(1, gz_count):
        pl.semaphore_signal(
            barrier, inc=1, device_id=(lax.rem(me + hop, gz_count), ph), device_id_type=MESH_ID
        )
    pl.semaphore_signal(barrier, inc=1, device_id=(me, other), device_id_type=MESH_ID)
    for fetch in fetches[4:]:
        fetch.start()

    radii = lax.broadcasted_iota(jnp.int32, (rows, around), 0).astype(jnp.float32) + 0.5
    row_id = lax.broadcasted_iota(jnp.int32, (rows, around), 0)
    lane = lax.broadcasted_iota(jnp.int32, (rows, half), 1)

    fetches[0].wait()
    wall = wall_ref[...].astype(jnp.float32)

    def rotate(z, carry):
        turn = offsets_ref[lax.rem(me * planes + z, axial_total)]
        fluid[z] = pltpu.roll(wall, turn, 1)
        return carry

    lax.fori_loop(0, planes + 1, rotate, 0)
    for fetch in fetches[1:4]:
        fetch.wait()
    size = diameters_ref[map_ref[0]]

    def opens(z):
        here = fluid[z]
        open_radial = jnp.where(row_id == rows - 1, 0.0, here * pltpu.roll(here, rows - 1, 0))
        open_around = here * pltpu.roll(here, around - 1, 1)
        return open_radial, open_around, here * fluid[z + 1]

    weight = -jnp.sqrt(radii) / DT_STEP
    share = 1.0 / lax.axis_size("ph")

    def source(z):
        volume = frac_ref[0, z].astype(jnp.float32)
        gas = [gas_ref[a, z].astype(jnp.float32) for a in range(3)]
        slip = [velocity_ref[0, a, z].astype(jnp.float32) - gas[a] for a in range(3)]
        speed = jnp.sqrt(1.0 + (slip[0] * slip[0] + slip[1] * slip[1] + slip[2] * slip[2]))
        beta = DRAG_SCALE * volume / (size * size) * (1.0 + 0.15 * speed)
        relax = 1.0 / (1.0 + DT_STEP * beta)
        open_radial, open_around, open_axial = opens(z)
        for a in range(3):
            pred[a, z] = gas[a] + relax * slip[a]
        pull = volume * relax
        flux_radial = (pull * slip[0] + share * gas[0]) * open_radial
        flux_around = (pull * slip[1] + share * gas[1]) * open_around
        flux_axial = (pull * slip[2] + share * gas[2]) * open_axial
        out = (radii + 0.5) * flux_radial
        inward = jnp.where(row_id == 0, 0.0, pltpu.roll(out, 1, 0))
        total = (out - inward) / radii
        total = total + (flux_around - pltpu.roll(flux_around, 1, 1)) / (radii * angle_step)
        term[z] = (total + flux_axial) * weight
        return flux_axial

    def swap(z):
        return pltpu.make_async_remote_copy(
            src_ref=modes.at[other, z],
            dst_ref=partner.at[z],
            send_sem=swap_send,
            recv_sem=swap_recv.at[z],
            device_id=(me, other),
            device_id_type=MESH_ID,
        )

    def to_modes(z, behind):
        out = triple_dot(term[z] - behind * weight, ahead_ref[0], ahead_ref[1])
        modes[0, z] = out[:, :half]
        modes[1, z] = out[:, half:]
        swap(z).start()

    axial_flux[...] = source(planes - 1)
    fetches[4].wait()
    pl.semaphore_wait(barrier, gz_count)
    halo_copy = pltpu.make_async_remote_copy(
        src_ref=axial_flux,
        dst_ref=halo,
        send_sem=halo_sem.at[0],
        recv_sem=halo_sem.at[1],
        device_id=(lax.rem(me + 1, gz_count), ph),
        device_id_type=MESH_ID,
    )
    halo_copy.start()

    def send_modes(k, carry):
        z = planes - 2 - k
        to_modes(z + 1, source(z))
        return carry

    lax.fori_loop(0, planes - 1, send_modes, 0)
    halo_copy.wait()
    to_modes(0, halo[...])

    for fetch in fetches[5:]:
        fetch.wait()

    def apply(table, loads):
        def add(k, accs):
            accs = list(accs)
            for j in range(8):
                r = k * 8 + j
                part = table[pl.ds(pl.multiple_of(r * rows, rows), rows), :]
                for i, load in enumerate(loads):
                    accs[i] = accs[i] + part * jnp.broadcast_to(load(r), (rows, half))
            return tuple(accs)

        zero = jnp.zeros((rows, half), jnp.float32)
        return lax.fori_loop(0, rows // 8, add, (zero,) * len(loads))

    def patch(which, h, x, out):
        exact = left_triple(nyquist_ref[0, which], nyquist_ref[1, which], x)
        return jnp.where(lane + (1 - h) == 0, exact, out)

    def share_lines(z, h):
        return pltpu.make_async_remote_copy(
            src_ref=lines.at[h, z],
            dst_ref=lines.at[h, z],
            send_sem=lines_sem.at[0],
            recv_sem=lines_sem.at[1],
            device_id=(me, other),
            device_id_type=MESH_ID,
        )

    def forward(k, carry):
        z = planes - 1 - k
        swap(z).wait_recv()
        x = modes[ph, z] + partner[z]
        partner[z] = x
        (out,) = apply(radial, [lambda r: partner[z, pl.ds(r, 1), :]])
        lines[ph, z] = patch(0, ph, x, out)
        share_lines(z, ph).start()
        return carry

    lax.fori_loop(0, planes, forward, 0)

    ratio = line_ref[ph, 0]
    rising = lines[ph, 0]
    for z in range(1, planes):
        rising = rising * ratio + lines[ph, z]
    falling = lines[ph, planes - 1]
    for z in range(planes - 2, -1, -1):
        falling = falling * ratio + lines[ph, z]
    for j in range(blocks):
        ends_out[j] = rising[8 * j : 8 * j + 8]
        ends_out[blocks + j] = falling[8 * j : 8 * j + 8]

    def give_ends(hop):
        to = lax.rem(me + hop, gz_count)
        return pltpu.make_async_remote_copy(
            src_ref=ends_out.at[to],
            dst_ref=ends_in.at[me],
            send_sem=ends_sem.at[0],
            recv_sem=ends_sem.at[1],
            device_id=(to, ph),
            device_id_type=MESH_ID,
        )

    def give_states(hop):
        to = lax.rem(me + hop, gz_count)
        return pltpu.make_async_remote_copy(
            src_ref=states_out.at[to],
            dst_ref=states_in.at[ph, me],
            send_sem=states_send,
            recv_sem=states_recv.at[hop],
            device_id=(to, ph),
            device_id_type=MESH_ID,
        )

    def relay(at, h):
        return pltpu.make_async_remote_copy(
            src_ref=states_in.at[h, at],
            dst_ref=states_in.at[h, at],
            send_sem=relay_sem.at[0],
            recv_sem=relay_sem.at[1],
            device_id=(me, other),
            device_id_type=MESH_ID,
        )

    def whole(ref, send, recv):
        return pltpu.make_async_remote_copy(
            src_ref=ref,
            dst_ref=ref,
            send_sem=send,
            recv_sem=recv,
            device_id=(me, other),
            device_id_type=MESH_ID,
        )

    sent_ends = whole(ends_in.at[pl.ds(0, gz_count - 1)], ends_sem.at[0], ends_sem.at[1])
    sent_lines = whole(lines.at[other], lines_sem.at[0], lines_sem.at[1])
    sent_relay = whole(states_in.at[other], relay_sem.at[0], relay_sem.at[1])

    for hop in range(1, gz_count):
        give_ends(hop).start()
    ends_in[me] = ends_out[me]

    def flip(l, carry):
        radial_back[pl.ds(pl.multiple_of(l * rows, rows), rows), :] = radial[
            pl.ds(l, rows, stride=rows), :
        ]
        return carry

    lax.fori_loop(0, rows, flip, 0)
    sent_ends.wait_recv()

    is_rise = 1 - me // blocks
    mine = lax.rem(me, blocks)
    jump = line_ref[ph, 2, pl.ds(pl.multiple_of(mine * 8, 8), 8), :]
    wrap = line_ref[ph, 3, pl.ds(pl.multiple_of(mine * 8, 8), 8), :]
    order = [is_rise * s + (1 - is_rise) * (gz_count - 1 - s) for s in range(gz_count)]
    state = jnp.zeros((8, half), jnp.float32)
    for s in range(gz_count):
        state = state * jump + ends_in[order[s]]
    state = state * wrap
    for s in range(gz_count):
        states_out[order[s]] = state
        state = state * jump + ends_in[order[s]]

    for hop in range(1, gz_count):
        give_states(hop).start()
    states_in[ph, me] = states_out[me]
    relay(me, ph).start()
    for hop in range(1, gz_count):
        give_states(hop).wait_recv()
        relay(lax.rem(me + gz_count - hop, gz_count), ph).start()

    def solve(h):
        ratio = line_ref[h, 0]
        scale = line_ref[h, 1]
        right = jnp.concatenate([states_in[h, blocks + j] for j in range(blocks)], 0)
        left = jnp.concatenate([states_in[h, j] for j in range(blocks)], 0)
        last = right
        behind = right * ratio
        for z in range(planes - 1, -1, -1):
            solved[z] = behind
            behind = (behind + lines[h, z]) * ratio
        for z in range(planes):
            left = left * ratio + lines[h, z]
            solved[z] = (solved[z] + left) * scale
        solved[planes] = (last + left * ratio) * scale

    shrink = 1.0 / jnp.sqrt(radii[:, :half])

    def inverse(h, k):
        at = [k * group + i for i in range(group)]
        outs = apply(radial_back, [lambda r, z=z: solved[z, pl.ds(r, 1), :] for z in at])
        outs = [patch(1, h, solved[z], out) * shrink for z, out in zip(at, outs)]
        whole_rows = jnp.concatenate(outs, 0)
        found = triple_dot(whole_rows, back_ref[0, h], back_ref[1, h])
        return [found[i * rows : (i + 1) * rows] for i in range(group)]

    solve(ph)

    def own_half(k, carry):
        for i, part in enumerate(inverse(ph, k)):
            space[k * group + i] = part
        return carry

    lax.fori_loop(0, (planes + 1) // group, own_half, 0)

    sent_lines.wait_recv()
    sent_relay.wait_recv()
    solve(other)
    arc = 1.0 / (radii * angle_step)

    def correct(z):
        here = space[z]
        pressure_ref[z] = here
        open_radial, open_around, open_axial = opens(z)
        radial_step = (pltpu.roll(here, rows - 1, 0) - here) * open_radial
        around_step = (pltpu.roll(here, around - 1, 1) - here) * arc * open_around
        axial_step = (space[z + 1] - here) * open_axial
        for a, step in enumerate((radial_step, around_step, axial_step)):
            corrected_ref[0, a, z] = (pred[a, z] - DT_STEP * step).astype(jnp.bfloat16)

    for k in range((planes + 1) // group):
        for i, part in enumerate(inverse(other, k)):
            space[k * group + i] = space[k * group + i] + part
        for z in range(max(k * group - 1, 0), (k + 1) * group - 1):
            correct(z)

    whole(modes.at[other], swap_send, swap_recv.at[0]).wait_send()
    sent_lines.wait_send()
    sent_ends.wait_send()
    whole(states_out.at[pl.ds(0, gz_count - 1)], states_send, states_recv.at[0]).wait_send()
    sent_relay.wait_send()


def drum_step(gz_count, frac, velocity, gas_vel, diameters, phase_map, wall_mask, offsets):
    planes, rows, around = frac.shape[1:]
    half = around // 2
    first, nyquist, line, ahead, back = operator_tables(rows, around, offsets.shape[0], planes)
    smem = pl.BlockSpec(memory_space=pltpu.SMEM)
    f32 = jnp.float32
    dma = pltpu.SemaphoreType.DMA
    ends = (gz_count, 8, half)
    group = 3 if (planes + 1) % 3 == 0 else 1
    return pl.pallas_call(
        functools.partial(drum_kernel, gz_count, group),
        out_shape=(
            pltpu.VMEM((planes, rows, around), f32),
            pltpu.VMEM((1, 3, planes, rows, around), jnp.bfloat16),
        ),
        in_specs=[smem] * 3 + [pl.BlockSpec(memory_space=pl.ANY)] * 9,
        out_specs=[pl.BlockSpec(memory_space=pltpu.VMEM)] * 2,
        scratch_shapes=[
            pltpu.VMEM(wall_mask.shape, jnp.int32),
            pltpu.VMEM(frac.shape, jnp.bfloat16),
            pltpu.VMEM(velocity.shape, jnp.bfloat16),
            pltpu.VMEM(gas_vel.shape, jnp.bfloat16),
            pltpu.VMEM(ahead.shape, jnp.bfloat16),
            pltpu.VMEM(nyquist.shape, jnp.bfloat16),
            pltpu.VMEM(line.shape, f32),
            pltpu.VMEM(back.shape, jnp.bfloat16),
            pltpu.VMEM((rows * rows, half), f32),
            pltpu.VMEM((rows * rows, half), f32),
            pltpu.VMEM((planes + 1, rows, around), f32),
            pltpu.VMEM((3, planes, rows, around), f32),
            pltpu.VMEM((planes, rows, around), f32),
            pltpu.VMEM((rows, around), f32),
            pltpu.VMEM((rows, around), f32),
            pltpu.VMEM((2, planes, rows, half), f32),
            pltpu.VMEM((planes, rows, half), f32),
            pltpu.VMEM((2, planes, rows, half), f32),
            pltpu.VMEM(ends, f32),
            pltpu.VMEM(ends, f32),
            pltpu.VMEM(ends, f32),
            pltpu.VMEM((2, *ends), f32),
            pltpu.VMEM((planes + 1, rows, half), f32),
            pltpu.VMEM((planes + 1, rows, around), f32),
            dma((9,)),
            dma((2,)),
            dma,
            dma((planes,)),
            dma((2,)),
            dma((2,)),
            dma,
            dma((gz_count,)),
            dma((2,)),
        ],
        compiler_params=pltpu.CompilerParams(
            collective_id=0, has_side_effects=True, vmem_limit_bytes=56 * 1024 * 1024
        ),
    )(
        offsets,
        diameters,
        phase_map,
        wall_mask,
        frac,
        velocity,
        gas_vel,
        jnp.asarray(ahead),
        jnp.asarray(nyquist),
        jnp.asarray(line),
        jnp.asarray(back),
        jnp.asarray(first.reshape(rows * rows, half)),
    )


def solution(mesh):
    in_specs = (
        P("ph", "gz", None, None),
        P("ph", None, "gz", None, None),
        P(None, "gz", None, None),
        P(),
        P("ph"),
        P(),
        P(),
    )
    out_specs = (P("gz", None, None), P("ph", None, "gz", None, None))
    gz_count, ph_count = mesh.shape["gz"], mesh.shape["ph"]

    def body(frac, *rest):
        rows, around = frac.shape[2:]
        fits = ph_count == 2 and around == 256 and rows <= 128
        if fits and rows * 2 == gz_count * 8 and frac.shape[1] <= 8:
            return drum_step(gz_count, frac, *rest)
        return shards(frac, *rest)

    return jax.shard_map(body, mesh=mesh, in_specs=in_specs, out_specs=out_specs, check_vma=False)
```

```python
import functools
import math

import jax
import jax.numpy as jnp
import numpy as np
from jax import lax
from jax.experimental import pallas as pl
from jax.experimental.pallas import tpu as pltpu
from jax.sharding import PartitionSpec as P

DT_STEP = 0.5
DRAG_SCALE = 20.0
COMPRESS = 0.005
HIGHEST = lax.Precision.HIGHEST


def from_behind(block, axis, distance):
    devices = range(lax.axis_size(axis))
    route = [((i - distance) % len(devices), i) for i in devices]
    return lax.ppermute(block, axis, route)


def real_basis(count):
    index_rows = jnp.arange(count, dtype=jnp.int32)[:, None]
    column = jnp.arange(count, dtype=jnp.int32)[None, :]
    half = count // 2
    wave = jnp.where(column <= half, column, column - half)
    angle = 2.0 * math.pi / count * (index_rows * wave % count).astype(jnp.float32)
    scaled = math.sqrt(2.0 / count)
    cosine = jnp.cos(angle)
    table = jnp.where(column < half, scaled * cosine, scaled * jnp.sin(angle))
    return jnp.where((column == 0) | (column == half), cosine / math.sqrt(count), table)


def eigen_values(count):
    column = jnp.arange(count, dtype=jnp.int32)
    half = count // 2
    wave = jnp.where(column <= half, column, column - half).astype(jnp.float32)
    return 2.0 - 2.0 * jnp.cos(2.0 * math.pi / count * wave)


def rotate_mask(wall_mask, turns, around_count):
    around_idx = (
        jnp.arange(around_count, dtype=jnp.int32)[None, :] - turns[:, None]
    ) % around_count
    return jnp.transpose(jnp.take(wall_mask, around_idx, axis=1), (1, 0, 2)).astype(jnp.float32)


def radial_solve(spectral, axial_eig, theta_eig, radius_vec, angle_step):
    radial_count = radius_vec.shape[0]
    inner = radius_vec - 0.5
    outer = jnp.where(jnp.arange(radial_count) == radial_count - 1, 0.0, radius_vec + 0.5)
    diag = (
        COMPRESS
        + axial_eig[:, None, None]
        + theta_eig[None, :, None] / (radius_vec * angle_step) ** 2
        + ((outer + inner) / radius_vec)[None, None, :]
    )
    lower = jnp.broadcast_to(-inner / radius_vec, diag.shape)
    upper = jnp.broadcast_to(-outer / radius_vec, diag.shape)
    right = -jnp.transpose(spectral, (0, 2, 1))[..., None]
    solved = lax.linalg.tridiagonal_solve(lower, diag, upper, right)[..., 0]
    return jnp.transpose(solved, (0, 2, 1))


def to_space(modes, around_table):
    return jnp.dot(
        modes.reshape(-1, around_table.shape[0]), around_table.T, precision=HIGHEST
    ).reshape(modes.shape)


def shards(frac, velocity, gas_vel, diameters, phase_map, wall_mask, offsets):
    plane_count = frac.shape[1]
    radial_count = frac.shape[2]
    around_count = frac.shape[3]
    axial_total = offsets.shape[0]
    phase_count = lax.axis_size("ph")
    slab_index = lax.axis_index("gz")
    first_plane = slab_index * plane_count
    angle_step = 2.0 * math.pi / around_count
    plane_ids = (first_plane + jnp.arange(plane_count + 1, dtype=jnp.int32)) % axial_total
    fluid_all = rotate_mask(wall_mask, jnp.take(offsets, plane_ids), around_count)
    fluid = fluid_all[:plane_count]
    open_radial = fluid * jnp.concatenate([fluid[:, 1:], jnp.zeros_like(fluid[:, :1])], 1)
    open_around = fluid * jnp.roll(fluid, -1, 2)
    open_axial = fluid * fluid_all[1:]
    radius_vec = jnp.arange(radial_count, dtype=jnp.float32) + 0.5
    radii = radius_vec[:, None]
    which = (jnp.arange(diameters.shape[0], dtype=jnp.int32) == phase_map[0]).astype(jnp.float32)
    size_here = jnp.sum(diameters * which)
    volume = frac[0].astype(jnp.float32)
    gas = gas_vel.astype(jnp.float32)
    slip = velocity[0].astype(jnp.float32) - gas
    speed = jnp.sqrt(1.0 + jnp.sum(slip * slip, 0))
    beta = DRAG_SCALE * volume / (size_here * size_here) * (1.0 + 0.15 * speed)
    relax = 1.0 / (1.0 + DT_STEP * beta)
    predicted = gas + relax * slip
    share = volume * relax * slip + gas / phase_count
    flux_radial = share[0] * open_radial
    flux_around = share[1] * open_around
    flux_axial = share[2] * open_axial
    below = from_behind(flux_axial[-1:], "gz", 1)
    axial_prev = jnp.concatenate([below, flux_axial[:-1]], 0)
    radial_prev = jnp.concatenate([jnp.zeros_like(flux_radial[:, :1]), flux_radial[:, :-1]], 1)
    term = ((radii + 0.5) * flux_radial - (radii - 0.5) * radial_prev) / radii
    term = term + (flux_around - jnp.roll(flux_around, 1, 2)) / (radii * angle_step)
    term = (term + flux_axial - axial_prev) / DT_STEP
    around_table = real_basis(around_count)
    axial_table = real_basis(axial_total)
    axial_eig = eigen_values(axial_total)
    axial_step = None
    source = lax.psum(term, "ph")
    modes = jnp.dot(source.reshape(-1, around_count), around_table, precision=HIGHEST).reshape(
        source.shape
    )
    pencil = lax.all_to_all(modes, "gz", split_axis=2, concat_axis=0, tiled=True)
    mode_count = pencil.shape[2]
    theta_eig = lax.dynamic_slice_in_dim(
        eigen_values(around_count), slab_index * mode_count, mode_count
    )
    flat = pencil.reshape(axial_total, -1)
    spectral = jnp.dot(axial_table.T, flat, precision=HIGHEST).reshape(pencil.shape)
    solved = radial_solve(spectral, axial_eig, theta_eig, radius_vec, angle_step)
    space = jnp.dot(axial_table, solved.reshape(axial_total, -1), precision=HIGHEST).reshape(
        pencil.shape
    )
    ahead = jnp.roll(space, -1, 0) - space
    back, back_step = (
        lax.all_to_all(space, "gz", split_axis=0, concat_axis=2, tiled=True),
        lax.all_to_all(ahead, "gz", split_axis=0, concat_axis=2, tiled=True),
    )
    pressure = to_space(back, around_table)
    axial_step = to_space(back_step, around_table)
    radial_step = (jnp.concatenate([pressure[:, 1:], pressure[:, -1:]], 1) - pressure) * open_radial
    around_step = (jnp.roll(pressure, -1, 2) - pressure) / (radii * angle_step) * open_around
    gradient = jnp.stack([radial_step, around_step, axial_step * open_axial])
    corrected = (predicted - DT_STEP * gradient).astype(jnp.bfloat16)[None]
    return (pressure, corrected)


MESH_ID = pl.DeviceIdType.MESH


def split_low(x):
    high = x.astype(jnp.bfloat16)
    return high, (x - high.astype(jnp.float32)).astype(jnp.bfloat16)


def triple_dot(x, table_high, table_low):
    high, low = split_low(x)
    out = jnp.dot(high, table_high, preferred_element_type=jnp.float32)
    out = out + jnp.dot(low, table_high, preferred_element_type=jnp.float32)
    return out + jnp.dot(high, table_low, preferred_element_type=jnp.float32)


def np_high_low(table):
    high = table.astype(jnp.bfloat16)
    low = (table - high.astype(np.float64)).astype(jnp.bfloat16)
    return high, low


@functools.lru_cache(maxsize=None)
def operator_tables(radial, around, axial, planes):
    half = around // 2
    rows = np.arange(around)[:, None]
    column = np.arange(around)[None, :]
    wave = np.where(column <= half, column, column - half)
    angle = 2.0 * np.pi / around * (rows * wave % around)
    basis = np.sqrt(2.0 / around) * np.where(column <= half, np.cos(angle), np.sin(angle))
    basis = np.where((column == 0) | (column == half), np.cos(angle) / np.sqrt(around), basis)
    radius = np.arange(radial) + 0.5
    inner = radius - 0.5
    outer = np.where(np.arange(radial) == radial - 1, 0.0, radius + 0.5)
    step = 2.0 * np.pi / around
    vectors, values = [], []
    for m in range(half + 1):
        eig = 2.0 - 2.0 * np.cos(2.0 * np.pi / around * m)
        matrix = np.diag((outer + inner) / radius + eig / (radius * step) ** 2)
        off = -outer[:-1] / np.sqrt(radius[:-1] * radius[1:])
        matrix = matrix + np.diag(off, 1) + np.diag(off, -1)
        value, vector = np.linalg.eigh(matrix)
        vector = vector * np.where(vector[:1] < 0.0, -1.0, 1.0)
        values.append(value)
        vectors.append(vector)
    vectors = np.stack(vectors, -1)
    values = np.maximum(np.stack(values, -1), 0.0)
    first = vectors[:, :, :half]
    last = vectors[:, :, half]
    other = np.concatenate([values[:, half:], values[:, 1:half]], -1)
    over = COMPRESS + np.stack([values[:, :half], other])
    root = np.sqrt(over * (over + 4.0))
    ratio = 2.0 / (2.0 + over + root)
    jump = ratio**planes
    wrap = 1.0 / (1.0 - ratio**axial)
    line = np.stack([ratio, 1.0 / root, jump, wrap], 1).astype(np.float32)
    ahead = np_high_low(basis)
    back = np_high_low(basis.T.reshape(2, half, around))
    nyquist = np_high_low(last.T)
    fill = np.zeros((radial, max(radial, 128)))
    fill[:, :radial] = last / np.sqrt(radius)[:, None]
    return (
        first.astype(np.float32),
        np.stack(nyquist),
        fill.astype(np.float32),
        line,
        np.stack(ahead),
        np.stack(back),
    )


def left_triple(table_high, table_low, x):
    high, low = split_low(x)
    out = jnp.dot(table_high, high, preferred_element_type=jnp.float32)
    out = out + jnp.dot(table_high, low, preferred_element_type=jnp.float32)
    return out + jnp.dot(table_low, high, preferred_element_type=jnp.float32)


def drum_kernel(
    gz_count,
    group,
    offsets_ref,
    diameters_ref,
    map_ref,
    wall_hbm,
    frac_hbm,
    velocity_hbm,
    gas_hbm,
    ahead_hbm,
    nyquist_hbm,
    fill_hbm,
    line_hbm,
    back_hbm,
    radial_hbm,
    pressure_ref,
    corrected_ref,
    wall_ref,
    frac_ref,
    velocity_ref,
    gas_ref,
    ahead_ref,
    nyquist_ref,
    fill_ref,
    line_ref,
    back_ref,
    radial,
    radial_back,
    fluid,
    pred,
    gates,
    term,
    axial_flux,
    halo,
    modes,
    partner,
    lines,
    ends_out,
    ends_in,
    states_out,
    states_in,
    solved,
    result,
    space,
    input_sem,
    halo_sem,
    swap_send,
    swap_recv,
    lines_sem,
    ends_sem,
    states_send,
    states_recv,
    relay_sem,
):
    me = lax.axis_index("gz")
    ph = lax.axis_index("ph")
    other = 1 - ph
    planes, rows, around = term.shape
    half = around // 2
    axial_total = offsets_ref.shape[0]
    owners = gz_count // 2
    base = gz_count // 4
    width = ends_in.shape[1]
    blocks = owners // 2
    angle_step = 2.0 * math.pi / around

    pairs = (
        (wall_hbm, wall_ref),
        (frac_hbm, frac_ref),
        (velocity_hbm, velocity_ref),
        (gas_hbm, gas_ref),
        (ahead_hbm, ahead_ref),
        (radial_hbm, radial),
        (nyquist_hbm, nyquist_ref),
        (fill_hbm, fill_ref),
        (line_hbm, line_ref),
        (back_hbm, back_ref),
    )
    fetches = [pltpu.make_async_copy(a, b, input_sem.at[i]) for i, (a, b) in enumerate(pairs)]
    for fetch in fetches[:4]:
        fetch.start()
    barrier = pltpu.get_barrier_semaphore()
    for hop in range(1, gz_count):
        pl.semaphore_signal(
            barrier, inc=1, device_id=(lax.rem(me + hop, gz_count), ph), device_id_type=MESH_ID
        )
    pl.semaphore_signal(barrier, inc=1, device_id=(me, other), device_id_type=MESH_ID)
    for fetch in fetches[4:]:
        fetch.start()

    radii = lax.broadcasted_iota(jnp.int32, (rows, around), 0).astype(jnp.float32) + 0.5
    row_id = lax.broadcasted_iota(jnp.int32, (rows, around), 0)
    lane = lax.broadcasted_iota(jnp.int32, (rows, half), 1)

    fetches[0].wait()

    def rotate(z):
        turn = offsets_ref[lax.rem(me * planes + z, axial_total)]
        fluid[z] = pltpu.roll(wall_ref[...].astype(jnp.float32), turn, 1)

    rotate(planes)
    for fetch in fetches[1:4]:
        fetch.wait()
    size = diameters_ref[map_ref[0]]

    arc = 1.0 / (radii * angle_step)

    def opens(z):
        rotate(z)
        here = fluid[z]
        open_radial = jnp.where(row_id == rows - 1, 0.0, here * pltpu.roll(here, rows - 1, 0))
        open_around = here * pltpu.roll(here, around - 1, 1)
        return open_radial, open_around, here * fluid[z + 1]

    weight = -jnp.sqrt(radii) / DT_STEP
    share = 1.0 / lax.axis_size("ph")

    def source(z):
        volume = frac_ref[0, z].astype(jnp.float32)
        gas = [gas_ref[a, z].astype(jnp.float32) for a in range(3)]
        slip = [velocity_ref[0, a, z].astype(jnp.float32) - gas[a] for a in range(3)]
        speed = jnp.sqrt(1.0 + (slip[0] * slip[0] + slip[1] * slip[1] + slip[2] * slip[2]))
        beta = DRAG_SCALE * volume / (size * size) * (1.0 + 0.15 * speed)
        relax = 1.0 / (1.0 + DT_STEP * beta)
        open_radial, open_around, open_axial = opens(z)
        for a in range(3):
            pred[a, z] = gas[a] + relax * slip[a]
        gates[0, z] = DT_STEP * open_radial
        gates[1, z] = (DT_STEP * arc) * open_around
        gates[2, z] = DT_STEP * open_axial
        pull = volume * relax
        flux_radial = (pull * slip[0] + share * gas[0]) * open_radial
        flux_around = (pull * slip[1] + share * gas[1]) * open_around
        flux_axial = (pull * slip[2] + share * gas[2]) * open_axial
        out = (radii + 0.5) * flux_radial
        inward = jnp.where(row_id == 0, 0.0, pltpu.roll(out, 1, 0))
        total = (out - inward) / radii
        total = total + (flux_around - pltpu.roll(flux_around, 1, 1)) * arc
        term[z] = (total + flux_axial) * weight
        return flux_axial

    def swap(z):
        return pltpu.make_async_remote_copy(
            src_ref=modes.at[other, z],
            dst_ref=partner.at[z],
            send_sem=swap_send,
            recv_sem=swap_recv.at[z],
            device_id=(me, other),
            device_id_type=MESH_ID,
        )

    def to_modes(z, behind):
        out = triple_dot(term[z] - behind * weight, ahead_ref[0], ahead_ref[1])
        modes[0, z] = out[:, :half]
        modes[1, z] = out[:, half:]
        swap(z).start()

    axial_flux[...] = source(planes - 1)
    fetches[4].wait()
    pl.semaphore_wait(barrier, gz_count)
    halo_copy = pltpu.make_async_remote_copy(
        src_ref=axial_flux,
        dst_ref=halo,
        send_sem=halo_sem.at[0],
        recv_sem=halo_sem.at[1],
        device_id=(lax.rem(me + 1, gz_count), ph),
        device_id_type=MESH_ID,
    )
    halo_copy.start()

    def send_modes(k, carry):
        z = planes - 2 - k
        to_modes(z + 1, source(z))
        return carry

    lax.fori_loop(0, planes - 1, send_modes, 0)
    halo_copy.wait()
    to_modes(0, halo[...])

    for fetch in fetches[5:]:
        fetch.wait()

    def apply(table, loads):
        def add(k, accs):
            accs = list(accs)
            for j in range(8):
                r = k * 8 + j
                part = table[pl.ds(pl.multiple_of(r * rows, rows), rows), :]
                for i, load in enumerate(loads):
                    accs[i] = accs[i] + part * jnp.broadcast_to(load(r), (rows, half))
            return tuple(accs)

        zero = jnp.zeros((rows, half), jnp.float32)
        return lax.fori_loop(0, rows // 8, add, (zero,) * len(loads))

    def forward(k, carry):
        z = planes - 1 - k
        swap(z).wait_recv()
        x = modes[ph, z] + partner[z]
        partner[z] = x
        (out,) = apply(radial, [lambda r: partner[z, pl.ds(r, 1), :]])
        exact = left_triple(nyquist_ref[0], nyquist_ref[1], x)
        lines[ph, z] = jnp.where(lane + other == 0, exact, out)
        return carry

    lax.fori_loop(0, planes, forward, 0)

    ratio = line_ref[ph, 0]
    rising = lines[ph, 0]
    for z in range(1, planes):
        rising = rising * ratio + lines[ph, z]
    falling = lines[ph, planes - 1]
    for z in range(planes - 2, -1, -1):
        falling = falling * ratio + lines[ph, z]
    for j in range(blocks):
        ends_out[j] = rising[width * j : width * j + width]
        ends_out[blocks + j] = falling[width * j : width * j + width]

    is_owner = (me >= base) & (me < base + owners)

    def give_ends(o):
        return pltpu.make_async_remote_copy(
            src_ref=ends_out.at[o],
            dst_ref=ends_in.at[me],
            send_sem=ends_sem.at[0],
            recv_sem=ends_sem.at[1],
            device_id=(base + o, ph),
            device_id_type=MESH_ID,
        )

    def give_states(to, o):
        return pltpu.make_async_remote_copy(
            src_ref=states_out.at[to],
            dst_ref=states_in.at[ph, o],
            send_sem=states_send,
            recv_sem=states_recv.at[o],
            device_id=(to, ph),
            device_id_type=MESH_ID,
        )

    def relay(at, h):
        return pltpu.make_async_remote_copy(
            src_ref=states_in.at[h, at],
            dst_ref=states_in.at[h, at],
            send_sem=relay_sem.at[0],
            recv_sem=relay_sem.at[1],
            device_id=(me, other),
            device_id_type=MESH_ID,
        )

    def whole(ref, send, recv):
        return pltpu.make_async_remote_copy(
            src_ref=ref,
            dst_ref=ref,
            send_sem=send,
            recv_sem=recv,
            device_id=(me, other),
            device_id_type=MESH_ID,
        )

    sent_ends = whole(ends_in.at[pl.ds(0, gz_count - 1)], ends_sem.at[0], ends_sem.at[1])
    sent_relay = whole(states_in.at[other], relay_sem.at[0], relay_sem.at[1])
    late = me // (gz_count // 2)

    for k in range(owners):
        o = lax.rem(k + (1 - late) * blocks, owners)

        @pl.when(base + o != me)
        def _(o=o):
            give_ends(o).start()

    share_lines = whole(lines.at[ph], lines_sem.at[0], lines_sem.at[1])
    share_lines.start()

    @pl.when(is_owner)
    def _():
        ends_in[me] = ends_out[me - base]

    shrink = 1.0 / jnp.sqrt(radii[:, :half])

    def flip(l, carry):
        at = pl.ds(pl.multiple_of(l * rows, rows), rows)
        radial_back[0, at, :] = radial[pl.ds(l, rows, stride=rows), :] * shrink
        return carry

    lax.fori_loop(0, rows, flip, 0)

    @pl.when(is_owner)
    def _():
        sent_ends.wait_recv()
        mine = me - base
        is_rise = 1 - mine // blocks
        at = pl.ds(pl.multiple_of(lax.rem(mine, blocks) * width, width), width)
        jump = line_ref[ph, 2, at, :]
        wrap = line_ref[ph, 3, at, :]
        order = [is_rise * s + (1 - is_rise) * (gz_count - 1 - s) for s in range(gz_count)]
        state = jnp.zeros((width, half), jnp.float32)
        for s in range(gz_count):
            state = state * jump + ends_in[order[s]]
        state = state * wrap
        for s in range(gz_count):
            states_out[order[s]] = state
            state = state * jump + ends_in[order[s]]
        for hop in sorted(range(1, gz_count), key=lambda hop: abs(hop - gz_count // 2)):
            give_states(lax.rem(me + hop, gz_count), mine).start()
        states_in[ph, mine] = states_out[me]

    for l in range(rows):
        at = pl.ds(l * rows, rows)
        fill = jnp.broadcast_to(fill_ref[:, l : l + 1], (rows, half))
        radial_back[1, at, :] = jnp.where(lane == 0, fill, radial_back[0, at, :])

    for k in range(owners):
        o = lax.rem(k + late * blocks, owners)

        @pl.when(base + o != me)
        def _(o=o):
            give_states(me, o).wait_recv()

        relay(o, ph).start()

    def solve(h):
        ratio = line_ref[h, 0]
        scale = line_ref[h, 1]
        right = jnp.concatenate([states_in[h, blocks + j] for j in range(blocks)], 0)
        left = jnp.concatenate([states_in[h, j] for j in range(blocks)], 0)
        last = right
        behind = right * ratio
        for z in range(planes - 1, -1, -1):
            solved[z] = behind
            behind = (behind + lines[h, z]) * ratio
        for z in range(planes):
            left = left * ratio + lines[h, z]
            solved[z] = (solved[z] + left) * scale
        solved[planes] = (last + left * ratio) * scale

    groups = (planes + 1) // group

    def inverse(h, k):
        loads = [lambda r, z=k * group + i: solved[z, pl.ds(r, 1), :] for i in range(group)]
        return apply(radial_back.at[h], loads)

    solve(ph)

    def own_half(k, carry):
        for i, out in enumerate(inverse(ph, k)):
            result[k * group + i] = out
        return carry

    lax.fori_loop(0, groups, own_half, 0)

    share_lines.wait_recv()
    sent_relay.wait_recv()
    solve(other)

    def correct(z):
        here = space[z]
        pressure_ref[z] = here
        radial_step = (pltpu.roll(here, rows - 1, 0) - here) * gates[0, z]
        around_step = (pltpu.roll(here, around - 1, 1) - here) * gates[1, z]
        axial_step = (space[z + 1] - here) * gates[2, z]
        for a, step in enumerate((radial_step, around_step, axial_step)):
            corrected_ref[0, a, z] = (pred[a, z] - step).astype(jnp.bfloat16)

    for k in range(groups):
        outs = inverse(other, k)
        own = jnp.concatenate([result[k * group + i] for i in range(group)], 0)
        both = jnp.concatenate([own, jnp.concatenate(outs, 0)], 1)
        table = [jnp.concatenate([back_ref[i, ph], back_ref[i, other]], 0) for i in range(2)]
        found = triple_dot(both, *table)
        for z in range(max((k - 1) * group - 1, 0), k * group - 1):
            correct(z)
        for i in range(group):
            space[k * group + i] = found[i * rows : (i + 1) * rows]
    for z in range(max((groups - 1) * group - 1, 0), planes):
        correct(z)

    whole(modes.at[other], swap_send, swap_recv.at[0]).wait_send()
    share_lines.wait_send()
    sent_relay.wait_send()

    @pl.when(is_owner)
    def _():
        whole(ends_out.at[pl.ds(0, owners - 1)], ends_sem.at[0], ends_sem.at[1]).wait_send()
        sent = states_out.at[pl.ds(0, gz_count - 1)]
        whole(sent, states_send, states_recv.at[0]).wait_send()

    @pl.when(jnp.logical_not(is_owner))
    def _():
        whole(ends_out, ends_sem.at[0], ends_sem.at[1]).wait_send()


def put_kernel(pressure_vmem, corrected_vmem, pressure_out, corrected_out, sem):
    pairs = ((pressure_vmem, pressure_out), (corrected_vmem, corrected_out))
    copies = [pltpu.make_async_copy(a, b, sem.at[i]) for i, (a, b) in enumerate(pairs)]
    for copy in copies:
        copy.start()
    for copy in copies:
        copy.wait()


def drum_step(gz_count, frac, velocity, gas_vel, diameters, phase_map, wall_mask, offsets):
    planes, rows, around = frac.shape[1:]
    half = around // 2
    first, nyquist, fill, line, ahead, back = operator_tables(rows, around, offsets.shape[0], planes)
    smem = pl.BlockSpec(memory_space=pltpu.SMEM)
    f32 = jnp.float32
    dma = pltpu.SemaphoreType.DMA
    owners = gz_count // 2
    width = 2 * rows // owners
    group = 3 if (planes + 1) % 3 == 0 else 1
    results = pl.pallas_call(
        functools.partial(drum_kernel, gz_count, group),
        out_shape=(
            pltpu.VMEM((planes, rows, around), f32),
            pltpu.VMEM((1, 3, planes, rows, around), jnp.bfloat16),
        ),
        in_specs=[smem] * 3 + [pl.BlockSpec(memory_space=pl.ANY)] * 10,
        out_specs=[pl.BlockSpec(memory_space=pltpu.VMEM)] * 2,
        scratch_shapes=[
            pltpu.VMEM(wall_mask.shape, jnp.int32),
            pltpu.VMEM(frac.shape, jnp.bfloat16),
            pltpu.VMEM(velocity.shape, jnp.bfloat16),
            pltpu.VMEM(gas_vel.shape, jnp.bfloat16),
            pltpu.VMEM(ahead.shape, jnp.bfloat16),
            pltpu.VMEM(nyquist.shape, jnp.bfloat16),
            pltpu.VMEM(fill.shape, f32),
            pltpu.VMEM(line.shape, f32),
            pltpu.VMEM(back.shape, jnp.bfloat16),
            pltpu.VMEM((rows * rows, half), f32),
            pltpu.VMEM((2, rows * rows, half), f32),
            pltpu.VMEM((planes + 1, rows, around), f32),
            pltpu.VMEM((3, planes, rows, around), f32),
            pltpu.VMEM((3, planes, rows, around), f32),
            pltpu.VMEM((planes, rows, around), f32),
            pltpu.VMEM((rows, around), f32),
            pltpu.VMEM((rows, around), f32),
            pltpu.VMEM((2, planes, rows, half), f32),
            pltpu.VMEM((planes, rows, half), f32),
            pltpu.VMEM((2, planes, rows, half), f32),
            pltpu.VMEM((owners, width, half), f32),
            pltpu.VMEM((gz_count, width, half), f32),
            pltpu.VMEM((gz_count, width, half), f32),
            pltpu.VMEM((2, owners, width, half), f32),
            pltpu.VMEM((planes + 1, rows, half), f32),
            pltpu.VMEM((planes + 1, rows, half), f32),
            pltpu.VMEM((planes + 1, rows, around), f32),
            dma((10,)),
            dma((2,)),
            dma,
            dma((planes,)),
            dma((2,)),
            dma((2,)),
            dma,
            dma((owners,)),
            dma((2,)),
        ],
        compiler_params=pltpu.CompilerParams(
            collective_id=0, has_side_effects=True, vmem_limit_bytes=56 * 1024 * 1024
        ),
    )(
        offsets,
        diameters,
        phase_map,
        wall_mask,
        frac,
        velocity,
        gas_vel,
        jnp.asarray(ahead),
        jnp.asarray(nyquist),
        jnp.asarray(fill),
        jnp.asarray(line),
        jnp.asarray(back),
        jnp.asarray(first.reshape(rows * rows, half)),
    )
    return pl.pallas_call(
        put_kernel,
        out_shape=tuple(jax.ShapeDtypeStruct(x.shape, x.dtype) for x in results),
        in_specs=[pl.BlockSpec(memory_space=pltpu.VMEM)] * 2,
        out_specs=[pl.BlockSpec(memory_space=pl.ANY)] * 2,
        scratch_shapes=[dma((2,))],
        compiler_params=pltpu.CompilerParams(vmem_limit_bytes=4 * 1024 * 1024),
    )(*(pltpu.with_memory_space_constraint(x, pltpu.VMEM) for x in results))


def solution(mesh):
    in_specs = (
        P("ph", "gz", None, None),
        P("ph", None, "gz", None, None),
        P(None, "gz", None, None),
        P(),
        P("ph"),
        P(),
        P(),
    )
    out_specs = (P("gz", None, None), P("ph", None, "gz", None, None))
    gz_count, ph_count = mesh.shape["gz"], mesh.shape["ph"]

    def body(frac, *rest):
        rows, around = frac.shape[2:]
        fits = ph_count == 2 and around == 256 and rows <= 128 and gz_count % 4 == 0
        if fits and rows * 2 == gz_count * 8 and frac.shape[1] <= 8:
            return drum_step(gz_count, frac, *rest)
        return shards(frac, *rest)

    return jax.shard_map(body, mesh=mesh, in_specs=in_specs, out_specs=out_specs, check_vma=False)
```

```python
import functools
import math

import jax
import jax.numpy as jnp
import numpy as np
from jax import lax
from jax.experimental import pallas as pl
from jax.experimental.pallas import tpu as pltpu
from jax.sharding import PartitionSpec as P

DT_STEP = 0.5
DRAG_SCALE = 20.0
COMPRESS = 0.005
HIGHEST = lax.Precision.HIGHEST


def from_behind(block, axis, distance):
    devices = range(lax.axis_size(axis))
    route = [((i - distance) % len(devices), i) for i in devices]
    return lax.ppermute(block, axis, route)


def real_basis(count):
    index_rows = jnp.arange(count, dtype=jnp.int32)[:, None]
    column = jnp.arange(count, dtype=jnp.int32)[None, :]
    half = count // 2
    wave = jnp.where(column <= half, column, column - half)
    angle = 2.0 * math.pi / count * (index_rows * wave % count).astype(jnp.float32)
    scaled = math.sqrt(2.0 / count)
    cosine = jnp.cos(angle)
    table = jnp.where(column < half, scaled * cosine, scaled * jnp.sin(angle))
    return jnp.where((column == 0) | (column == half), cosine / math.sqrt(count), table)


def eigen_values(count):
    column = jnp.arange(count, dtype=jnp.int32)
    half = count // 2
    wave = jnp.where(column <= half, column, column - half).astype(jnp.float32)
    return 2.0 - 2.0 * jnp.cos(2.0 * math.pi / count * wave)


def rotate_mask(wall_mask, turns, around_count):
    around_idx = (
        jnp.arange(around_count, dtype=jnp.int32)[None, :] - turns[:, None]
    ) % around_count
    return jnp.transpose(jnp.take(wall_mask, around_idx, axis=1), (1, 0, 2)).astype(jnp.float32)


def radial_solve(spectral, axial_eig, theta_eig, radius_vec, angle_step):
    radial_count = radius_vec.shape[0]
    inner = radius_vec - 0.5
    outer = jnp.where(jnp.arange(radial_count) == radial_count - 1, 0.0, radius_vec + 0.5)
    diag = (
        COMPRESS
        + axial_eig[:, None, None]
        + theta_eig[None, :, None] / (radius_vec * angle_step) ** 2
        + ((outer + inner) / radius_vec)[None, None, :]
    )
    lower = jnp.broadcast_to(-inner / radius_vec, diag.shape)
    upper = jnp.broadcast_to(-outer / radius_vec, diag.shape)
    right = -jnp.transpose(spectral, (0, 2, 1))[..., None]
    solved = lax.linalg.tridiagonal_solve(lower, diag, upper, right)[..., 0]
    return jnp.transpose(solved, (0, 2, 1))


def to_space(modes, around_table):
    return jnp.dot(
        modes.reshape(-1, around_table.shape[0]), around_table.T, precision=HIGHEST
    ).reshape(modes.shape)


def shards(frac, velocity, gas_vel, diameters, phase_map, wall_mask, offsets):
    plane_count = frac.shape[1]
    radial_count = frac.shape[2]
    around_count = frac.shape[3]
    axial_total = offsets.shape[0]
    phase_count = lax.axis_size("ph")
    slab_index = lax.axis_index("gz")
    first_plane = slab_index * plane_count
    angle_step = 2.0 * math.pi / around_count
    plane_ids = (first_plane + jnp.arange(plane_count + 1, dtype=jnp.int32)) % axial_total
    fluid_all = rotate_mask(wall_mask, jnp.take(offsets, plane_ids), around_count)
    fluid = fluid_all[:plane_count]
    open_radial = fluid * jnp.concatenate([fluid[:, 1:], jnp.zeros_like(fluid[:, :1])], 1)
    open_around = fluid * jnp.roll(fluid, -1, 2)
    open_axial = fluid * fluid_all[1:]
    radius_vec = jnp.arange(radial_count, dtype=jnp.float32) + 0.5
    radii = radius_vec[:, None]
    which = (jnp.arange(diameters.shape[0], dtype=jnp.int32) == phase_map[0]).astype(jnp.float32)
    size_here = jnp.sum(diameters * which)
    volume = frac[0].astype(jnp.float32)
    gas = gas_vel.astype(jnp.float32)
    slip = velocity[0].astype(jnp.float32) - gas
    speed = jnp.sqrt(1.0 + jnp.sum(slip * slip, 0))
    beta = DRAG_SCALE * volume / (size_here * size_here) * (1.0 + 0.15 * speed)
    relax = 1.0 / (1.0 + DT_STEP * beta)
    predicted = gas + relax * slip
    share = volume * relax * slip + gas / phase_count
    flux_radial = share[0] * open_radial
    flux_around = share[1] * open_around
    flux_axial = share[2] * open_axial
    below = from_behind(flux_axial[-1:], "gz", 1)
    axial_prev = jnp.concatenate([below, flux_axial[:-1]], 0)
    radial_prev = jnp.concatenate([jnp.zeros_like(flux_radial[:, :1]), flux_radial[:, :-1]], 1)
    term = ((radii + 0.5) * flux_radial - (radii - 0.5) * radial_prev) / radii
    term = term + (flux_around - jnp.roll(flux_around, 1, 2)) / (radii * angle_step)
    term = (term + flux_axial - axial_prev) / DT_STEP
    around_table = real_basis(around_count)
    axial_table = real_basis(axial_total)
    axial_eig = eigen_values(axial_total)
    axial_step = None
    source = lax.psum(term, "ph")
    modes = jnp.dot(source.reshape(-1, around_count), around_table, precision=HIGHEST).reshape(
        source.shape
    )
    pencil = lax.all_to_all(modes, "gz", split_axis=2, concat_axis=0, tiled=True)
    mode_count = pencil.shape[2]
    theta_eig = lax.dynamic_slice_in_dim(
        eigen_values(around_count), slab_index * mode_count, mode_count
    )
    flat = pencil.reshape(axial_total, -1)
    spectral = jnp.dot(axial_table.T, flat, precision=HIGHEST).reshape(pencil.shape)
    solved = radial_solve(spectral, axial_eig, theta_eig, radius_vec, angle_step)
    space = jnp.dot(axial_table, solved.reshape(axial_total, -1), precision=HIGHEST).reshape(
        pencil.shape
    )
    ahead = jnp.roll(space, -1, 0) - space
    back, back_step = (
        lax.all_to_all(space, "gz", split_axis=0, concat_axis=2, tiled=True),
        lax.all_to_all(ahead, "gz", split_axis=0, concat_axis=2, tiled=True),
    )
    pressure = to_space(back, around_table)
    axial_step = to_space(back_step, around_table)
    radial_step = (jnp.concatenate([pressure[:, 1:], pressure[:, -1:]], 1) - pressure) * open_radial
    around_step = (jnp.roll(pressure, -1, 2) - pressure) / (radii * angle_step) * open_around
    gradient = jnp.stack([radial_step, around_step, axial_step * open_axial])
    corrected = (predicted - DT_STEP * gradient).astype(jnp.bfloat16)[None]
    return (pressure, corrected)


MESH_ID = pl.DeviceIdType.MESH


def split_low(x):
    high = x.astype(jnp.bfloat16)
    return high, (x - high.astype(jnp.float32)).astype(jnp.bfloat16)


def triple_dot(x, table_high, table_low):
    high, low = split_low(x)
    out = jnp.dot(high, table_high, preferred_element_type=jnp.float32)
    out = out + jnp.dot(low, table_high, preferred_element_type=jnp.float32)
    return out + jnp.dot(high, table_low, preferred_element_type=jnp.float32)


def np_high_low(table):
    high = table.astype(jnp.bfloat16)
    low = (table - high.astype(np.float64)).astype(jnp.bfloat16)
    return high, low


@functools.lru_cache(maxsize=None)
def operator_tables(radial, around, axial, planes):
    half = around // 2
    rows = np.arange(around)[:, None]
    column = np.arange(around)[None, :]
    wave = np.where(column <= half, column, column - half)
    angle = 2.0 * np.pi / around * (rows * wave % around)
    basis = np.sqrt(2.0 / around) * np.where(column <= half, np.cos(angle), np.sin(angle))
    basis = np.where((column == 0) | (column == half), np.cos(angle) / np.sqrt(around), basis)
    radius = np.arange(radial) + 0.5
    inner = radius - 0.5
    outer = np.where(np.arange(radial) == radial - 1, 0.0, radius + 0.5)
    step = 2.0 * np.pi / around
    vectors, values = [], []
    for m in range(half + 1):
        eig = 2.0 - 2.0 * np.cos(2.0 * np.pi / around * m)
        matrix = np.diag((outer + inner) / radius + eig / (radius * step) ** 2)
        off = -outer[:-1] / np.sqrt(radius[:-1] * radius[1:])
        matrix = matrix + np.diag(off, 1) + np.diag(off, -1)
        value, vector = np.linalg.eigh(matrix)
        vector = vector * np.where(vector[:1] < 0.0, -1.0, 1.0)
        values.append(value)
        vectors.append(vector)
    vectors = np.stack(vectors, -1)
    values = np.maximum(np.stack(values, -1), 0.0)
    first = vectors[:, :, :half]
    last = vectors[:, :, half]
    other = np.concatenate([values[:, half:], values[:, 1:half]], -1)
    over = COMPRESS + np.stack([values[:, :half], other])
    root = np.sqrt(over * (over + 4.0))
    ratio = 2.0 / (2.0 + over + root)
    jump = ratio**planes
    wrap = 1.0 / (1.0 - ratio**axial)
    line = np.stack([ratio, 1.0 / root, jump, wrap], 1).astype(np.float32)
    ahead = np_high_low(basis)
    back = np_high_low(basis.T.reshape(2, half, around))
    nyquist = np_high_low(last.T)
    fill = np.zeros((radial, max(radial, 128)))
    fill[:, :radial] = last / np.sqrt(radius)[:, None]
    return (
        first.astype(np.float32),
        np.stack(nyquist),
        fill.astype(np.float32),
        line,
        np.stack(ahead),
        np.stack(back),
    )


def left_triple(table_high, table_low, x):
    high, low = split_low(x)
    out = jnp.dot(table_high, high, preferred_element_type=jnp.float32)
    out = out + jnp.dot(table_high, low, preferred_element_type=jnp.float32)
    return out + jnp.dot(table_low, high, preferred_element_type=jnp.float32)


def drum_kernel(
    gz_count,
    offsets_ref,
    diameters_ref,
    map_ref,
    wall_hbm,
    frac_hbm,
    velocity_hbm,
    gas_hbm,
    ahead_hbm,
    nyquist_hbm,
    fill_hbm,
    line_hbm,
    back_hbm,
    radial_hbm,
    pressure_ref,
    corrected_ref,
    wall_ref,
    frac_ref,
    velocity_ref,
    gas_ref,
    ahead_ref,
    nyquist_ref,
    fill_ref,
    line_ref,
    back_ref,
    radial,
    radial_back,
    fluid,
    pred,
    gates,
    term,
    axial_flux,
    halo,
    modes,
    partner,
    lines,
    ends_out,
    ends_in,
    states_out,
    states_in,
    solved,
    result,
    space,
    input_sem,
    halo_sem,
    swap_send,
    swap_recv,
    lines_sem,
    ends_sem,
    states_send,
    states_recv,
    relay_sem,
    known_sem,
):
    me = lax.axis_index("gz")
    ph = lax.axis_index("ph")
    other = 1 - ph
    planes, rows, around = term.shape
    half = around // 2
    axial_total = offsets_ref.shape[0]
    owners = gz_count // 2
    base = gz_count // 4
    width = ends_in.shape[1]
    blocks = owners // 2
    angle_step = 2.0 * math.pi / around

    last = planes - 1
    streams = ((frac_hbm, frac_ref), (velocity_hbm, velocity_ref), (gas_hbm, gas_ref))

    def part(ref, start, count):
        lead = (slice(None),) * (len(ref.shape) - 3)
        return ref.at[(*lead, pl.ds(start, count))]

    tables = (
        (ahead_hbm, ahead_ref),
        (radial_hbm, radial),
        (nyquist_hbm, nyquist_ref),
        (fill_hbm, fill_ref),
        (line_hbm, line_ref),
        (back_hbm, back_ref),
    )
    pairs = [(part(a, last, 1), part(b, last, 1)) for a, b in streams]
    pairs += [(wall_hbm, wall_ref)]
    pairs += [(part(a, 0, last), part(b, 0, last)) for a, b in streams]
    pairs += tables
    fetches = [pltpu.make_async_copy(a, b, input_sem.at[i]) for i, (a, b) in enumerate(pairs)]
    barrier = pltpu.get_barrier_semaphore()
    for fetch in fetches[:4]:
        fetch.start()
    for to in ((lax.rem(me + 1, gz_count), ph), (lax.rem(me + gz_count - 1, gz_count), ph)):
        pl.semaphore_signal(barrier, inc=1, device_id=to, device_id_type=MESH_ID)
    pl.semaphore_signal(barrier, inc=1, device_id=(me, other), device_id_type=MESH_ID)
    for fetch in fetches[4:8]:
        fetch.start()

    def greet(step):
        for to in (me + 2**step, me + gz_count - 2**step):
            pl.semaphore_signal(
                known_sem.at[step],
                inc=1,
                device_id=(lax.rem(to, gz_count), ph),
                device_id_type=MESH_ID,
            )

    steps = known_sem.shape[0]

    def spread(step):
        if step < steps:
            pl.semaphore_wait(known_sem.at[step], 2)
        if step + 1 < steps:
            greet(step + 1)

    radii = lax.broadcasted_iota(jnp.int32, (rows, around), 0).astype(jnp.float32) + 0.5
    row_id = lax.broadcasted_iota(jnp.int32, (rows, around), 0)
    lane = lax.broadcasted_iota(jnp.int32, (rows, half), 1)

    def rotate(z):
        turn = offsets_ref[lax.rem(me * planes + z, axial_total)]
        fluid[z] = pltpu.roll(wall_ref[...].astype(jnp.float32), turn, 1)

    for fetch in fetches[:4]:
        fetch.wait()
    rotate(planes)
    size = diameters_ref[map_ref[0]]

    arc = 1.0 / (radii * angle_step)

    def opens(z):
        rotate(z)
        here = fluid[z]
        open_radial = jnp.where(row_id == rows - 1, 0.0, here * pltpu.roll(here, rows - 1, 0))
        open_around = here * pltpu.roll(here, around - 1, 1)
        return open_radial, open_around, here * fluid[z + 1]

    weight = -jnp.sqrt(radii) / DT_STEP
    share = 1.0 / lax.axis_size("ph")

    def source(z):
        volume = frac_ref[0, z].astype(jnp.float32)
        gas = [gas_ref[a, z].astype(jnp.float32) for a in range(3)]
        slip = [velocity_ref[0, a, z].astype(jnp.float32) - gas[a] for a in range(3)]
        speed = jnp.sqrt(1.0 + (slip[0] * slip[0] + slip[1] * slip[1] + slip[2] * slip[2]))
        beta = DRAG_SCALE * volume / (size * size) * (1.0 + 0.15 * speed)
        relax = 1.0 / (1.0 + DT_STEP * beta)
        open_radial, open_around, open_axial = opens(z)
        for a in range(3):
            pred[a, z] = gas[a] + relax * slip[a]
        gates[0, z] = DT_STEP * open_radial
        gates[1, z] = (DT_STEP * arc) * open_around
        gates[2, z] = DT_STEP * open_axial
        pull = volume * relax
        flux_radial = (pull * slip[0] + share * gas[0]) * open_radial
        flux_around = (pull * slip[1] + share * gas[1]) * open_around
        flux_axial = (pull * slip[2] + share * gas[2]) * open_axial
        out = (radii + 0.5) * flux_radial
        inward = jnp.where(row_id == 0, 0.0, pltpu.roll(out, 1, 0))
        total = (out - inward) / radii
        total = total + (flux_around - pltpu.roll(flux_around, 1, 1)) * arc
        term[z] = (total + flux_axial) * weight
        return flux_axial

    def swap(z):
        return pltpu.make_async_remote_copy(
            src_ref=modes.at[other, z],
            dst_ref=partner.at[z],
            send_sem=swap_send,
            recv_sem=swap_recv.at[z],
            device_id=(me, other),
            device_id_type=MESH_ID,
        )

    def to_modes(z, behind):
        out = triple_dot(term[z] - behind * weight, ahead_ref[0], ahead_ref[1])
        modes[0, z] = out[:, :half]
        modes[1, z] = out[:, half:]
        swap(z).start()

    axial_flux[...] = source(last)
    for fetch in fetches[8:]:
        fetch.start()
    pl.semaphore_wait(barrier, 3)
    greet(0)
    halo_copy = pltpu.make_async_remote_copy(
        src_ref=axial_flux,
        dst_ref=halo,
        send_sem=halo_sem.at[0],
        recv_sem=halo_sem.at[1],
        device_id=(lax.rem(me + 1, gz_count), ph),
        device_id_type=MESH_ID,
    )
    halo_copy.start()
    for fetch in fetches[4:8]:
        fetch.wait()

    def send_modes(k, carry):
        z = planes - 2 - k
        to_modes(z + 1, source(z))
        return carry

    lax.fori_loop(0, planes - 1, send_modes, 0)
    halo_copy.wait()
    to_modes(0, halo[...])

    spread(0)
    for fetch in fetches[8:]:
        fetch.wait()

    def apply(table, loads):
        def add(k, accs):
            accs = list(accs)
            for j in range(8):
                r = k * 8 + j
                part = table[pl.ds(pl.multiple_of(r * rows, rows), rows), :]
                for i, load in enumerate(loads):
                    accs[i] = accs[i] + part * jnp.broadcast_to(load(r), (rows, half))
            return tuple(accs)

        zero = jnp.zeros((rows, half), jnp.float32)
        return lax.fori_loop(0, rows // 8, add, (zero,) * len(loads))

    def forward(k, carry):
        z = planes - 1 - k
        swap(z).wait_recv()
        x = modes[ph, z] + partner[z]
        partner[z] = x
        (out,) = apply(radial, [lambda r: partner[z, pl.ds(r, 1), :]])
        exact = left_triple(nyquist_ref[0], nyquist_ref[1], x)
        lines[ph, z] = jnp.where(lane + other == 0, exact, out)
        return carry

    lax.fori_loop(0, planes // 2, forward, 0)
    spread(1)
    lax.fori_loop(planes // 2, planes, forward, 0)
    for step in range(2, steps):
        spread(step)

    ratio = line_ref[ph, 0]
    rising = lines[ph, 0]
    for z in range(1, planes):
        rising = rising * ratio + lines[ph, z]
    falling = lines[ph, planes - 1]
    for z in range(planes - 2, -1, -1):
        falling = falling * ratio + lines[ph, z]
    for j in range(blocks):
        ends_out[j] = rising[width * j : width * j + width]
        ends_out[blocks + j] = falling[width * j : width * j + width]

    is_owner = (me >= base) & (me < base + owners)

    def give_ends(o):
        return pltpu.make_async_remote_copy(
            src_ref=ends_out.at[o],
            dst_ref=ends_in.at[me],
            send_sem=ends_sem.at[0],
            recv_sem=ends_sem.at[1],
            device_id=(base + o, ph),
            device_id_type=MESH_ID,
        )

    def give_states(to, o):
        return pltpu.make_async_remote_copy(
            src_ref=states_out.at[to],
            dst_ref=states_in.at[ph, o],
            send_sem=states_send,
            recv_sem=states_recv.at[o],
            device_id=(to, ph),
            device_id_type=MESH_ID,
        )

    def relay(at, h):
        return pltpu.make_async_remote_copy(
            src_ref=states_in.at[h, at],
            dst_ref=states_in.at[h, at],
            send_sem=relay_sem.at[0],
            recv_sem=relay_sem.at[1],
            device_id=(me, other),
            device_id_type=MESH_ID,
        )

    def whole(ref, send, recv):
        return pltpu.make_async_remote_copy(
            src_ref=ref,
            dst_ref=ref,
            send_sem=send,
            recv_sem=recv,
            device_id=(me, other),
            device_id_type=MESH_ID,
        )

    sent_ends = whole(ends_in.at[pl.ds(0, gz_count - 1)], ends_sem.at[0], ends_sem.at[1])
    sent_relay = whole(states_in.at[other], relay_sem.at[0], relay_sem.at[1])
    late = me // (gz_count // 2)

    for k in range(owners):
        side = 1 - late if k < blocks else late
        o = side * blocks + lax.rem(k + me, blocks)

        @pl.when(base + o != me)
        def _(o=o):
            give_ends(o).start()

    share_lines = whole(lines.at[ph], lines_sem.at[0], lines_sem.at[1])
    share_lines.start()

    @pl.when(is_owner)
    def _():
        ends_in[me] = ends_out[me - base]

    shrink = 1.0 / jnp.sqrt(radii[:, :half])

    def flip(l, carry):
        at = pl.ds(pl.multiple_of(l * rows, rows), rows)
        radial_back[0, at, :] = radial[pl.ds(l, rows, stride=rows), :] * shrink
        return carry

    lax.fori_loop(0, rows, flip, 0)

    @pl.when(is_owner)
    def _():
        sent_ends.wait_recv()
        mine = me - base
        is_rise = 1 - mine // blocks
        at = pl.ds(pl.multiple_of(lax.rem(mine, blocks) * width, width), width)
        jump = line_ref[ph, 2, at, :]
        wrap = line_ref[ph, 3, at, :]
        order = [is_rise * s + (1 - is_rise) * (gz_count - 1 - s) for s in range(gz_count)]
        state = jnp.zeros((width, half), jnp.float32)
        for s in range(gz_count):
            state = state * jump + ends_in[order[s]]
        state = state * wrap
        for s in range(gz_count):
            states_out[order[s]] = state
            state = state * jump + ends_in[order[s]]
        for hop in sorted(range(1, gz_count), key=lambda hop: abs(hop - gz_count // 2)):
            give_states(lax.rem(me + hop, gz_count), mine).start()
        states_in[ph, mine] = states_out[me]

    for l in range(rows):
        at = pl.ds(l * rows, rows)
        fill = jnp.broadcast_to(fill_ref[:, l : l + 1], (rows, half))
        radial_back[1, at, :] = jnp.where(lane == 0, fill, radial_back[0, at, :])

    for k in range(owners):
        o = lax.rem(k + late * blocks, owners)

        @pl.when(base + o != me)
        def _(o=o):
            give_states(me, o).wait_recv()

        relay(o, ph).start()

    def solve(h):
        ratio = line_ref[h, 0]
        scale = line_ref[h, 1]
        right = jnp.concatenate([states_in[h, blocks + j] for j in range(blocks)], 0)
        left = jnp.concatenate([states_in[h, j] for j in range(blocks)], 0)
        last = right
        behind = right * ratio
        for z in range(planes - 1, -1, -1):
            solved[z] = behind
            behind = (behind + lines[h, z]) * ratio
        for z in range(planes):
            left = left * ratio + lines[h, z]
            solved[z] = (solved[z] + left) * scale
        solved[planes] = (last + left * ratio) * scale

    left_over = list(range(planes + 1))
    groups = []
    while left_over:
        groups.append(left_over[-4:])
        left_over = left_over[:-4]

    def inverse(h, at):
        return apply(radial_back.at[h], [lambda r, z=z: solved[z, pl.ds(r, 1), :] for z in at])

    solve(ph)

    for at in groups:
        for z, out in zip(at, inverse(ph, at)):
            result[z] = out

    share_lines.wait_recv()
    sent_relay.wait_recv()
    solve(other)

    def correct(z):
        here = space[z]
        pressure_ref[z] = here
        radial_step = (pltpu.roll(here, rows - 1, 0) - here) * gates[0, z]
        around_step = (pltpu.roll(here, around - 1, 1) - here) * gates[1, z]
        axial_step = (space[z + 1] - here) * gates[2, z]
        for a, step in enumerate((radial_step, around_step, axial_step)):
            corrected_ref[0, a, z] = (pred[a, z] - step).astype(jnp.bfloat16)

    before = []
    for at in groups:
        outs = inverse(other, at)
        own = jnp.concatenate([result[z] for z in at], 0)
        both = jnp.concatenate([own, jnp.concatenate(outs, 0)], 1)
        table = [jnp.concatenate([back_ref[i, ph], back_ref[i, other]], 0) for i in range(2)]
        found = triple_dot(both, *table)
        for z in before:
            correct(z)
        for i, z in enumerate(at):
            space[z] = found[i * rows : (i + 1) * rows]
        before = [z for z in at if z < planes]
    for z in before:
        correct(z)

    whole(modes.at[other], swap_send, swap_recv.at[0]).wait_send()
    share_lines.wait_send()
    sent_relay.wait_send()

    @pl.when(is_owner)
    def _():
        whole(ends_out.at[pl.ds(0, owners - 1)], ends_sem.at[0], ends_sem.at[1]).wait_send()
        sent = states_out.at[pl.ds(0, gz_count - 1)]
        whole(sent, states_send, states_recv.at[0]).wait_send()

    @pl.when(jnp.logical_not(is_owner))
    def _():
        whole(ends_out, ends_sem.at[0], ends_sem.at[1]).wait_send()


def put_kernel(pressure_vmem, corrected_vmem, pressure_out, corrected_out, sem):
    planes = pressure_vmem.shape[0]
    for z in range(planes):
        pltpu.make_async_copy(pressure_vmem.at[z], pressure_out.at[z], sem.at[0]).start()
        at = (0, slice(None), z)
        pltpu.make_async_copy(corrected_vmem.at[at], corrected_out.at[at], sem.at[1]).start()
    pltpu.make_async_copy(pressure_vmem, pressure_out, sem.at[0]).wait()
    pltpu.make_async_copy(corrected_vmem, corrected_out, sem.at[1]).wait()


def drum_step(gz_count, frac, velocity, gas_vel, diameters, phase_map, wall_mask, offsets):
    planes, rows, around = frac.shape[1:]
    half = around // 2
    first, nyquist, fill, line, ahead, back = operator_tables(rows, around, offsets.shape[0], planes)
    smem = pl.BlockSpec(memory_space=pltpu.SMEM)
    f32 = jnp.float32
    dma = pltpu.SemaphoreType.DMA
    owners = gz_count // 2
    width = 2 * rows // owners
    results = pl.pallas_call(
        functools.partial(drum_kernel, gz_count),
        out_shape=(
            pltpu.VMEM((planes, rows, around), f32),
            pltpu.VMEM((1, 3, planes, rows, around), jnp.bfloat16),
        ),
        in_specs=[smem] * 3 + [pl.BlockSpec(memory_space=pl.ANY)] * 10,
        out_specs=[pl.BlockSpec(memory_space=pltpu.VMEM)] * 2,
        scratch_shapes=[
            pltpu.VMEM(wall_mask.shape, jnp.int32),
            pltpu.VMEM(frac.shape, jnp.bfloat16),
            pltpu.VMEM(velocity.shape, jnp.bfloat16),
            pltpu.VMEM(gas_vel.shape, jnp.bfloat16),
            pltpu.VMEM(ahead.shape, jnp.bfloat16),
            pltpu.VMEM(nyquist.shape, jnp.bfloat16),
            pltpu.VMEM(fill.shape, f32),
            pltpu.VMEM(line.shape, f32),
            pltpu.VMEM(back.shape, jnp.bfloat16),
            pltpu.VMEM((rows * rows, half), f32),
            pltpu.VMEM((2, rows * rows, half), f32),
            pltpu.VMEM((planes + 1, rows, around), f32),
            pltpu.VMEM((3, planes, rows, around), f32),
            pltpu.VMEM((3, planes, rows, around), f32),
            pltpu.VMEM((planes, rows, around), f32),
            pltpu.VMEM((rows, around), f32),
            pltpu.VMEM((rows, around), f32),
            pltpu.VMEM((2, planes, rows, half), f32),
            pltpu.VMEM((planes, rows, half), f32),
            pltpu.VMEM((2, planes, rows, half), f32),
            pltpu.VMEM((owners, width, half), f32),
            pltpu.VMEM((gz_count, width, half), f32),
            pltpu.VMEM((gz_count, width, half), f32),
            pltpu.VMEM((2, owners, width, half), f32),
            pltpu.VMEM((planes + 1, rows, half), f32),
            pltpu.VMEM((planes + 1, rows, half), f32),
            pltpu.VMEM((planes + 1, rows, around), f32),
            dma((13,)),
            dma((2,)),
            dma,
            dma((planes,)),
            dma((2,)),
            dma((2,)),
            dma,
            dma((owners,)),
            dma((2,)),
            pltpu.SemaphoreType.REGULAR(((gz_count // 2 - 1).bit_length(),)),
        ],
        compiler_params=pltpu.CompilerParams(
            collective_id=0, has_side_effects=True, vmem_limit_bytes=56 * 1024 * 1024
        ),
    )(
        offsets,
        diameters,
        phase_map,
        wall_mask,
        frac,
        velocity,
        gas_vel,
        jnp.asarray(ahead),
        jnp.asarray(nyquist),
        jnp.asarray(fill),
        jnp.asarray(line),
        jnp.asarray(back),
        jnp.asarray(first.reshape(rows * rows, half)),
    )
    return pl.pallas_call(
        put_kernel,
        out_shape=tuple(jax.ShapeDtypeStruct(x.shape, x.dtype) for x in results),
        in_specs=[pl.BlockSpec(memory_space=pltpu.VMEM)] * 2,
        out_specs=[pl.BlockSpec(memory_space=pl.ANY)] * 2,
        scratch_shapes=[dma((2,))],
        compiler_params=pltpu.CompilerParams(vmem_limit_bytes=4 * 1024 * 1024),
    )(*(pltpu.with_memory_space_constraint(x, pltpu.VMEM) for x in results))


def solution(mesh):
    in_specs = (
        P("ph", "gz", None, None),
        P("ph", None, "gz", None, None),
        P(None, "gz", None, None),
        P(),
        P("ph"),
        P(),
        P(),
    )
    out_specs = (P("gz", None, None), P("ph", None, "gz", None, None))
    gz_count, ph_count = mesh.shape["gz"], mesh.shape["ph"]

    def body(frac, *rest):
        rows, around = frac.shape[2:]
        fits = ph_count == 2 and around == 256 and rows <= 128 and gz_count % 4 == 0
        if fits and rows * 2 == gz_count * 8 and frac.shape[1] <= 8:
            return drum_step(gz_count, frac, *rest)
        return shards(frac, *rest)

    return jax.shard_map(body, mesh=mesh, in_specs=in_specs, out_specs=out_specs, check_vma=False)
```

```python
import functools
import math

import jax
import jax.numpy as jnp
import numpy as np
from jax import lax
from jax.experimental import pallas as pl
from jax.experimental.pallas import tpu as pltpu
from jax.sharding import PartitionSpec as P

DT_STEP = 0.5
DRAG_SCALE = 20.0
COMPRESS = 0.005
HIGHEST = lax.Precision.HIGHEST


def from_behind(block, axis, distance):
    devices = range(lax.axis_size(axis))
    route = [((i - distance) % len(devices), i) for i in devices]
    return lax.ppermute(block, axis, route)


def real_basis(count):
    index_rows = jnp.arange(count, dtype=jnp.int32)[:, None]
    column = jnp.arange(count, dtype=jnp.int32)[None, :]
    half = count // 2
    wave = jnp.where(column <= half, column, column - half)
    angle = 2.0 * math.pi / count * (index_rows * wave % count).astype(jnp.float32)
    scaled = math.sqrt(2.0 / count)
    cosine = jnp.cos(angle)
    table = jnp.where(column < half, scaled * cosine, scaled * jnp.sin(angle))
    return jnp.where((column == 0) | (column == half), cosine / math.sqrt(count), table)


def eigen_values(count):
    column = jnp.arange(count, dtype=jnp.int32)
    half = count // 2
    wave = jnp.where(column <= half, column, column - half).astype(jnp.float32)
    return 2.0 - 2.0 * jnp.cos(2.0 * math.pi / count * wave)


def rotate_mask(wall_mask, turns, around_count):
    around_idx = (
        jnp.arange(around_count, dtype=jnp.int32)[None, :] - turns[:, None]
    ) % around_count
    return jnp.transpose(jnp.take(wall_mask, around_idx, axis=1), (1, 0, 2)).astype(jnp.float32)


def radial_solve(spectral, axial_eig, theta_eig, radius_vec, angle_step):
    radial_count = radius_vec.shape[0]
    inner = radius_vec - 0.5
    outer = jnp.where(jnp.arange(radial_count) == radial_count - 1, 0.0, radius_vec + 0.5)
    diag = (
        COMPRESS
        + axial_eig[:, None, None]
        + theta_eig[None, :, None] / (radius_vec * angle_step) ** 2
        + ((outer + inner) / radius_vec)[None, None, :]
    )
    lower = jnp.broadcast_to(-inner / radius_vec, diag.shape)
    upper = jnp.broadcast_to(-outer / radius_vec, diag.shape)
    right = -jnp.transpose(spectral, (0, 2, 1))[..., None]
    solved = lax.linalg.tridiagonal_solve(lower, diag, upper, right)[..., 0]
    return jnp.transpose(solved, (0, 2, 1))


def to_space(modes, around_table):
    return jnp.dot(
        modes.reshape(-1, around_table.shape[0]), around_table.T, precision=HIGHEST
    ).reshape(modes.shape)


def shards(frac, velocity, gas_vel, diameters, phase_map, wall_mask, offsets):
    plane_count = frac.shape[1]
    radial_count = frac.shape[2]
    around_count = frac.shape[3]
    axial_total = offsets.shape[0]
    phase_count = lax.axis_size("ph")
    slab_index = lax.axis_index("gz")
    first_plane = slab_index * plane_count
    angle_step = 2.0 * math.pi / around_count
    plane_ids = (first_plane + jnp.arange(plane_count + 1, dtype=jnp.int32)) % axial_total
    fluid_all = rotate_mask(wall_mask, jnp.take(offsets, plane_ids), around_count)
    fluid = fluid_all[:plane_count]
    open_radial = fluid * jnp.concatenate([fluid[:, 1:], jnp.zeros_like(fluid[:, :1])], 1)
    open_around = fluid * jnp.roll(fluid, -1, 2)
    open_axial = fluid * fluid_all[1:]
    radius_vec = jnp.arange(radial_count, dtype=jnp.float32) + 0.5
    radii = radius_vec[:, None]
    which = (jnp.arange(diameters.shape[0], dtype=jnp.int32) == phase_map[0]).astype(jnp.float32)
    size_here = jnp.sum(diameters * which)
    volume = frac[0].astype(jnp.float32)
    gas = gas_vel.astype(jnp.float32)
    slip = velocity[0].astype(jnp.float32) - gas
    speed = jnp.sqrt(1.0 + jnp.sum(slip * slip, 0))
    beta = DRAG_SCALE * volume / (size_here * size_here) * (1.0 + 0.15 * speed)
    relax = 1.0 / (1.0 + DT_STEP * beta)
    predicted = gas + relax * slip
    share = volume * relax * slip + gas / phase_count
    flux_radial = share[0] * open_radial
    flux_around = share[1] * open_around
    flux_axial = share[2] * open_axial
    below = from_behind(flux_axial[-1:], "gz", 1)
    axial_prev = jnp.concatenate([below, flux_axial[:-1]], 0)
    radial_prev = jnp.concatenate([jnp.zeros_like(flux_radial[:, :1]), flux_radial[:, :-1]], 1)
    term = ((radii + 0.5) * flux_radial - (radii - 0.5) * radial_prev) / radii
    term = term + (flux_around - jnp.roll(flux_around, 1, 2)) / (radii * angle_step)
    term = (term + flux_axial - axial_prev) / DT_STEP
    around_table = real_basis(around_count)
    axial_table = real_basis(axial_total)
    axial_eig = eigen_values(axial_total)
    axial_step = None
    source = lax.psum(term, "ph")
    modes = jnp.dot(source.reshape(-1, around_count), around_table, precision=HIGHEST).reshape(
        source.shape
    )
    pencil = lax.all_to_all(modes, "gz", split_axis=2, concat_axis=0, tiled=True)
    mode_count = pencil.shape[2]
    theta_eig = lax.dynamic_slice_in_dim(
        eigen_values(around_count), slab_index * mode_count, mode_count
    )
    flat = pencil.reshape(axial_total, -1)
    spectral = jnp.dot(axial_table.T, flat, precision=HIGHEST).reshape(pencil.shape)
    solved = radial_solve(spectral, axial_eig, theta_eig, radius_vec, angle_step)
    space = jnp.dot(axial_table, solved.reshape(axial_total, -1), precision=HIGHEST).reshape(
        pencil.shape
    )
    ahead = jnp.roll(space, -1, 0) - space
    back, back_step = (
        lax.all_to_all(space, "gz", split_axis=0, concat_axis=2, tiled=True),
        lax.all_to_all(ahead, "gz", split_axis=0, concat_axis=2, tiled=True),
    )
    pressure = to_space(back, around_table)
    axial_step = to_space(back_step, around_table)
    radial_step = (jnp.concatenate([pressure[:, 1:], pressure[:, -1:]], 1) - pressure) * open_radial
    around_step = (jnp.roll(pressure, -1, 2) - pressure) / (radii * angle_step) * open_around
    gradient = jnp.stack([radial_step, around_step, axial_step * open_axial])
    corrected = (predicted - DT_STEP * gradient).astype(jnp.bfloat16)[None]
    return (pressure, corrected)


MESH_ID = pl.DeviceIdType.MESH


def split_low(x):
    high = x.astype(jnp.bfloat16)
    return high, (x - high.astype(jnp.float32)).astype(jnp.bfloat16)


def triple_dot(x, table_high, table_low):
    high, low = split_low(x)
    out = jnp.dot(high, table_high, preferred_element_type=jnp.float32)
    out = out + jnp.dot(low, table_high, preferred_element_type=jnp.float32)
    return out + jnp.dot(high, table_low, preferred_element_type=jnp.float32)


def np_high_low(table):
    high = table.astype(jnp.bfloat16)
    low = (table - high.astype(np.float64)).astype(jnp.bfloat16)
    return high, low


@functools.lru_cache(maxsize=None)
def operator_tables(radial, around, axial, planes):
    half = around // 2
    rows = np.arange(around)[:, None]
    column = np.arange(around)[None, :]
    wave = np.where(column <= half, column, column - half)
    angle = 2.0 * np.pi / around * (rows * wave % around)
    basis = np.sqrt(2.0 / around) * np.where(column <= half, np.cos(angle), np.sin(angle))
    basis = np.where((column == 0) | (column == half), np.cos(angle) / np.sqrt(around), basis)
    radius = np.arange(radial) + 0.5
    inner = radius - 0.5
    outer = np.where(np.arange(radial) == radial - 1, 0.0, radius + 0.5)
    step = 2.0 * np.pi / around
    vectors, values = [], []
    for m in range(half + 1):
        eig = 2.0 - 2.0 * np.cos(2.0 * np.pi / around * m)
        matrix = np.diag((outer + inner) / radius + eig / (radius * step) ** 2)
        off = -outer[:-1] / np.sqrt(radius[:-1] * radius[1:])
        matrix = matrix + np.diag(off, 1) + np.diag(off, -1)
        value, vector = np.linalg.eigh(matrix)
        vector = vector * np.where(vector[:1] < 0.0, -1.0, 1.0)
        values.append(value)
        vectors.append(vector)
    vectors = np.stack(vectors, -1)
    values = np.maximum(np.stack(values, -1), 0.0)
    first = vectors[:, :, :half]
    last = vectors[:, :, half]
    other = np.concatenate([values[:, half:], values[:, 1:half]], -1)
    over = COMPRESS + np.stack([values[:, :half], other])
    root = np.sqrt(over * (over + 4.0))
    ratio = 2.0 / (2.0 + over + root)
    jump = ratio**planes
    wrap = 1.0 / (1.0 - ratio**axial)
    line = np.stack([ratio, 1.0 / root, jump, wrap], 1).astype(np.float32)
    ahead = np_high_low(basis)
    back = np_high_low(basis.T.reshape(2, half, around))
    nyquist = np_high_low(last.T)
    fill = np.zeros((radial, max(radial, 128)))
    fill[:, :radial] = last / np.sqrt(radius)[:, None]
    return (
        first.astype(np.float32),
        np.stack(nyquist),
        fill.astype(np.float32),
        line,
        np.stack(ahead),
        np.stack(back),
    )


def left_triple(table_high, table_low, x):
    high, low = split_low(x)
    out = jnp.dot(table_high, high, preferred_element_type=jnp.float32)
    out = out + jnp.dot(table_high, low, preferred_element_type=jnp.float32)
    return out + jnp.dot(table_low, high, preferred_element_type=jnp.float32)


def drum_kernel(
    gz_count,
    offsets_hbm,
    diameters_hbm,
    map_hbm,
    wall_hbm,
    frac_hbm,
    velocity_hbm,
    gas_hbm,
    ahead_hbm,
    nyquist_hbm,
    fill_hbm,
    line_hbm,
    back_hbm,
    radial_hbm,
    pressure_ref,
    corrected_ref,
    offsets_ref,
    diameters_ref,
    map_ref,
    wall_ref,
    frac_ref,
    velocity_ref,
    gas_ref,
    ahead_ref,
    nyquist_ref,
    fill_ref,
    line_ref,
    back_ref,
    radial,
    radial_back,
    fluid,
    pred,
    gates,
    term,
    axial_flux,
    halo,
    modes,
    partner,
    lines,
    ends_out,
    ends_in,
    states_out,
    states_in,
    solved,
    result,
    space,
    scalar_sem,
    input_sem,
    halo_sem,
    swap_send,
    swap_recv,
    lines_sem,
    ends_sem,
    states_send,
    states_recv,
    relay_sem,
    known_sem,
):
    me = lax.axis_index("gz")
    ph = lax.axis_index("ph")
    other = 1 - ph
    planes, rows, around = term.shape
    half = around // 2
    axial_total = offsets_ref.shape[0]
    owners = gz_count // 2
    base = gz_count // 4
    width = ends_in.shape[1]
    blocks = owners // 2
    angle_step = 2.0 * math.pi / around

    last = planes - 1
    streams = ((frac_hbm, frac_ref), (velocity_hbm, velocity_ref), (gas_hbm, gas_ref))

    def part(ref, start, count):
        lead = (slice(None),) * (len(ref.shape) - 3)
        return ref.at[(*lead, pl.ds(start, count))]

    tables = (
        (ahead_hbm, ahead_ref),
        (radial_hbm, radial),
        (nyquist_hbm, nyquist_ref),
        (fill_hbm, fill_ref),
        (line_hbm, line_ref),
        (back_hbm, back_ref),
    )
    pairs = [(part(a, last, 1), part(b, last, 1)) for a, b in streams]
    pairs += [(wall_hbm, wall_ref)]
    pairs += [(part(a, 0, last), part(b, 0, last)) for a, b in streams]
    pairs += tables
    fetches = [pltpu.make_async_copy(a, b, input_sem.at[i]) for i, (a, b) in enumerate(pairs)]
    small = ((offsets_hbm, offsets_ref), (diameters_hbm, diameters_ref), (map_hbm, map_ref))
    scalars = [pltpu.make_async_copy(a, b, scalar_sem.at[i]) for i, (a, b) in enumerate(small)]
    barrier = pltpu.get_barrier_semaphore()
    for fetch in scalars + fetches[:4]:
        fetch.start()
    for to in ((lax.rem(me + 1, gz_count), ph), (lax.rem(me + gz_count - 1, gz_count), ph)):
        pl.semaphore_signal(barrier, inc=1, device_id=to, device_id_type=MESH_ID)
    pl.semaphore_signal(barrier, inc=1, device_id=(me, other), device_id_type=MESH_ID)
    for fetch in fetches[4:8]:
        fetch.start()

    def greet(step):
        for to in (me + 2**step, me + gz_count - 2**step):
            pl.semaphore_signal(
                known_sem.at[step],
                inc=1,
                device_id=(lax.rem(to, gz_count), ph),
                device_id_type=MESH_ID,
            )

    steps = known_sem.shape[0]

    def spread(step):
        if step < steps:
            pl.semaphore_wait(known_sem.at[step], 2)
        if step + 1 < steps:
            greet(step + 1)

    radii = lax.broadcasted_iota(jnp.int32, (rows, around), 0).astype(jnp.float32) + 0.5
    row_id = lax.broadcasted_iota(jnp.int32, (rows, around), 0)
    lane = lax.broadcasted_iota(jnp.int32, (rows, half), 1)

    def rotate(z):
        turn = offsets_ref[lax.rem(me * planes + z, axial_total)]
        fluid[z] = pltpu.roll(wall_ref[...].astype(jnp.float32), turn, 1)

    for fetch in scalars + fetches[:4]:
        fetch.wait()
    rotate(planes)
    size = diameters_ref[map_ref[0]]

    arc = 1.0 / (radii * angle_step)

    def opens(z):
        rotate(z)
        here = fluid[z]
        open_radial = jnp.where(row_id == rows - 1, 0.0, here * pltpu.roll(here, rows - 1, 0))
        open_around = here * pltpu.roll(here, around - 1, 1)
        return open_radial, open_around, here * fluid[z + 1]

    weight = -jnp.sqrt(radii) / DT_STEP
    share = 1.0 / lax.axis_size("ph")

    def source(z):
        volume = frac_ref[0, z].astype(jnp.float32)
        gas = [gas_ref[a, z].astype(jnp.float32) for a in range(3)]
        slip = [velocity_ref[0, a, z].astype(jnp.float32) - gas[a] for a in range(3)]
        speed = jnp.sqrt(1.0 + (slip[0] * slip[0] + slip[1] * slip[1] + slip[2] * slip[2]))
        beta = DRAG_SCALE * volume / (size * size) * (1.0 + 0.15 * speed)
        relax = 1.0 / (1.0 + DT_STEP * beta)
        open_radial, open_around, open_axial = opens(z)
        for a in range(3):
            pred[a, z] = gas[a] + relax * slip[a]
        gates[0, z] = DT_STEP * open_radial
        gates[1, z] = (DT_STEP * arc) * open_around
        gates[2, z] = DT_STEP * open_axial
        pull = volume * relax
        flux_radial = (pull * slip[0] + share * gas[0]) * open_radial
        flux_around = (pull * slip[1] + share * gas[1]) * open_around
        flux_axial = (pull * slip[2] + share * gas[2]) * open_axial
        out = (radii + 0.5) * flux_radial
        inward = jnp.where(row_id == 0, 0.0, pltpu.roll(out, 1, 0))
        total = (out - inward) / radii
        total = total + (flux_around - pltpu.roll(flux_around, 1, 1)) * arc
        term[z] = (total + flux_axial) * weight
        return flux_axial

    def swap(z):
        return pltpu.make_async_remote_copy(
            src_ref=modes.at[other, z],
            dst_ref=partner.at[z],
            send_sem=swap_send,
            recv_sem=swap_recv.at[z],
            device_id=(me, other),
            device_id_type=MESH_ID,
        )

    def to_modes(z, behind):
        out = triple_dot(term[z] - behind * weight, ahead_ref[0], ahead_ref[1])
        modes[0, z] = out[:, :half]
        modes[1, z] = out[:, half:]
        swap(z).start()

    axial_flux[...] = source(last)
    for fetch in fetches[8:]:
        fetch.start()
    pl.semaphore_wait(barrier, 3)
    greet(0)
    halo_copy = pltpu.make_async_remote_copy(
        src_ref=axial_flux,
        dst_ref=halo,
        send_sem=halo_sem.at[0],
        recv_sem=halo_sem.at[1],
        device_id=(lax.rem(me + 1, gz_count), ph),
        device_id_type=MESH_ID,
    )
    halo_copy.start()
    for fetch in fetches[4:8]:
        fetch.wait()

    def send_modes(k, carry):
        z = planes - 2 - k
        to_modes(z + 1, source(z))
        return carry

    lax.fori_loop(0, planes - 1, send_modes, 0)
    halo_copy.wait()
    to_modes(0, halo[...])

    spread(0)
    for fetch in fetches[8:]:
        fetch.wait()

    def apply(table, loads):
        def add(k, accs):
            accs = list(accs)
            for j in range(8):
                r = k * 8 + j
                part = table[pl.ds(pl.multiple_of(r * rows, rows), rows), :]
                for i, load in enumerate(loads):
                    accs[i] = accs[i] + part * jnp.broadcast_to(load(r), (rows, half))
            return tuple(accs)

        zero = jnp.zeros((rows, half), jnp.float32)
        return lax.fori_loop(0, rows // 8, add, (zero,) * len(loads))

    def forward(k, carry):
        z = planes - 1 - k
        swap(z).wait_recv()
        x = modes[ph, z] + partner[z]
        partner[z] = x
        (out,) = apply(radial, [lambda r: partner[z, pl.ds(r, 1), :]])
        exact = left_triple(nyquist_ref[0], nyquist_ref[1], x)
        lines[ph, z] = jnp.where(lane + other == 0, exact, out)
        return carry

    lax.fori_loop(0, planes // 2, forward, 0)
    spread(1)
    lax.fori_loop(planes // 2, planes, forward, 0)
    for step in range(2, steps):
        spread(step)

    ratio = line_ref[ph, 0]
    rising = lines[ph, 0]
    for z in range(1, planes):
        rising = rising * ratio + lines[ph, z]
    falling = lines[ph, planes - 1]
    for z in range(planes - 2, -1, -1):
        falling = falling * ratio + lines[ph, z]
    for j in range(blocks):
        ends_out[j] = rising[width * j : width * j + width]
        ends_out[blocks + j] = falling[width * j : width * j + width]

    is_owner = (me >= base) & (me < base + owners)

    def give_ends(o):
        return pltpu.make_async_remote_copy(
            src_ref=ends_out.at[o],
            dst_ref=ends_in.at[me],
            send_sem=ends_sem.at[0],
            recv_sem=ends_sem.at[1],
            device_id=(base + o, ph),
            device_id_type=MESH_ID,
        )

    def give_states(to, o):
        return pltpu.make_async_remote_copy(
            src_ref=states_out.at[to],
            dst_ref=states_in.at[ph, o],
            send_sem=states_send,
            recv_sem=states_recv.at[o],
            device_id=(to, ph),
            device_id_type=MESH_ID,
        )

    def relay(at, h):
        return pltpu.make_async_remote_copy(
            src_ref=states_in.at[h, at],
            dst_ref=states_in.at[h, at],
            send_sem=relay_sem.at[0],
            recv_sem=relay_sem.at[1],
            device_id=(me, other),
            device_id_type=MESH_ID,
        )

    def whole(ref, send, recv):
        return pltpu.make_async_remote_copy(
            src_ref=ref,
            dst_ref=ref,
            send_sem=send,
            recv_sem=recv,
            device_id=(me, other),
            device_id_type=MESH_ID,
        )

    sent_ends = whole(ends_in.at[pl.ds(0, gz_count - 1)], ends_sem.at[0], ends_sem.at[1])
    sent_relay = whole(states_in.at[other], relay_sem.at[0], relay_sem.at[1])
    late = me // (gz_count // 2)

    for k in range(owners):
        side = 1 - late if k < blocks else late
        o = side * blocks + lax.rem(k + me, blocks)

        @pl.when(base + o != me)
        def _(o=o):
            give_ends(o).start()

    share_lines = whole(lines.at[ph], lines_sem.at[0], lines_sem.at[1])
    share_lines.start()

    @pl.when(is_owner)
    def _():
        ends_in[me] = ends_out[me - base]

    shrink = 1.0 / jnp.sqrt(radii[:, :half])

    def flip(l, carry):
        at = pl.ds(pl.multiple_of(l * rows, rows), rows)
        radial_back[0, at, :] = radial[pl.ds(l, rows, stride=rows), :] * shrink
        return carry

    lax.fori_loop(0, rows, flip, 0)

    @pl.when(is_owner)
    def _():
        sent_ends.wait_recv()
        mine = me - base
        is_rise = 1 - mine // blocks
        at = pl.ds(pl.multiple_of(lax.rem(mine, blocks) * width, width), width)
        jump = line_ref[ph, 2, at, :]
        wrap = line_ref[ph, 3, at, :]
        order = [is_rise * s + (1 - is_rise) * (gz_count - 1 - s) for s in range(gz_count)]
        state = jnp.zeros((width, half), jnp.float32)
        for s in range(gz_count):
            state = state * jump + ends_in[order[s]]
        state = state * wrap
        for s in range(gz_count):
            states_out[order[s]] = state
            state = state * jump + ends_in[order[s]]
        for hop in sorted(range(1, gz_count), key=lambda hop: abs(hop - gz_count // 2)):
            give_states(lax.rem(me + hop, gz_count), mine).start()
        states_in[ph, mine] = states_out[me]

    for l in range(rows):
        at = pl.ds(l * rows, rows)
        fill = jnp.broadcast_to(fill_ref[:, l : l + 1], (rows, half))
        radial_back[1, at, :] = jnp.where(lane == 0, fill, radial_back[0, at, :])

    for k in range(owners):
        o = lax.rem(k + late * blocks, owners)

        @pl.when(base + o != me)
        def _(o=o):
            give_states(me, o).wait_recv()

        relay(o, ph).start()

    def solve(h):
        ratio = line_ref[h, 0]
        scale = line_ref[h, 1]
        right = jnp.concatenate([states_in[h, blocks + j] for j in range(blocks)], 0)
        left = jnp.concatenate([states_in[h, j] for j in range(blocks)], 0)
        last = right
        behind = right * ratio
        for z in range(planes - 1, -1, -1):
            solved[z] = behind
            behind = (behind + lines[h, z]) * ratio
        for z in range(planes):
            left = left * ratio + lines[h, z]
            solved[z] = (solved[z] + left) * scale
        solved[planes] = (last + left * ratio) * scale

    left_over = list(range(planes + 1))
    groups = []
    while left_over:
        groups.append(left_over[-4:])
        left_over = left_over[:-4]

    def inverse(h, at):
        return apply(radial_back.at[h], [lambda r, z=z: solved[z, pl.ds(r, 1), :] for z in at])

    solve(ph)

    for at in groups:
        for z, out in zip(at, inverse(ph, at)):
            result[z] = out

    share_lines.wait_recv()
    sent_relay.wait_recv()
    solve(other)

    def correct(z):
        here = space[z]
        pressure_ref[z] = here
        radial_step = (pltpu.roll(here, rows - 1, 0) - here) * gates[0, z]
        around_step = (pltpu.roll(here, around - 1, 1) - here) * gates[1, z]
        axial_step = (space[z + 1] - here) * gates[2, z]
        for a, step in enumerate((radial_step, around_step, axial_step)):
            corrected_ref[0, a, z] = (pred[a, z] - step).astype(jnp.bfloat16)

    before = []
    for at in groups:
        outs = inverse(other, at)
        own = jnp.concatenate([result[z] for z in at], 0)
        both = jnp.concatenate([own, jnp.concatenate(outs, 0)], 1)
        table = [jnp.concatenate([back_ref[i, ph], back_ref[i, other]], 0) for i in range(2)]
        found = triple_dot(both, *table)
        for z in before:
            correct(z)
        for i, z in enumerate(at):
            space[z] = found[i * rows : (i + 1) * rows]
        before = [z for z in at if z < planes]
    for z in before:
        correct(z)

    whole(modes.at[other], swap_send, swap_recv.at[0]).wait_send()
    share_lines.wait_send()
    sent_relay.wait_send()

    @pl.when(is_owner)
    def _():
        whole(ends_out.at[pl.ds(0, owners - 1)], ends_sem.at[0], ends_sem.at[1]).wait_send()
        sent = states_out.at[pl.ds(0, gz_count - 1)]
        whole(sent, states_send, states_recv.at[0]).wait_send()

    @pl.when(jnp.logical_not(is_owner))
    def _():
        whole(ends_out, ends_sem.at[0], ends_sem.at[1]).wait_send()


def put_kernel(pressure_vmem, corrected_vmem, pressure_out, corrected_out, sem):
    planes = pressure_vmem.shape[0]
    for z in range(planes):
        pltpu.make_async_copy(pressure_vmem.at[z], pressure_out.at[z], sem.at[0]).start()
        at = (0, slice(None), z)
        pltpu.make_async_copy(corrected_vmem.at[at], corrected_out.at[at], sem.at[1]).start()
    pltpu.make_async_copy(pressure_vmem, pressure_out, sem.at[0]).wait()
    pltpu.make_async_copy(corrected_vmem, corrected_out, sem.at[1]).wait()


def drum_step(gz_count, frac, velocity, gas_vel, diameters, phase_map, wall_mask, offsets):
    planes, rows, around = frac.shape[1:]
    half = around // 2
    first, nyquist, fill, line, ahead, back = operator_tables(rows, around, offsets.shape[0], planes)
    f32 = jnp.float32
    dma = pltpu.SemaphoreType.DMA
    owners = gz_count // 2
    width = 2 * rows // owners
    results = pl.pallas_call(
        functools.partial(drum_kernel, gz_count),
        out_shape=(
            pltpu.VMEM((planes, rows, around), f32),
            pltpu.VMEM((1, 3, planes, rows, around), jnp.bfloat16),
        ),
        in_specs=[pl.BlockSpec(memory_space=pl.ANY)] * 13,
        out_specs=[pl.BlockSpec(memory_space=pltpu.VMEM)] * 2,
        scratch_shapes=[
            pltpu.SMEM(offsets.shape, jnp.int32),
            pltpu.SMEM(diameters.shape, f32),
            pltpu.SMEM(phase_map.shape, jnp.int32),
            pltpu.VMEM(wall_mask.shape, jnp.int32),
            pltpu.VMEM(frac.shape, jnp.bfloat16),
            pltpu.VMEM(velocity.shape, jnp.bfloat16),
            pltpu.VMEM(gas_vel.shape, jnp.bfloat16),
            pltpu.VMEM(ahead.shape, jnp.bfloat16),
            pltpu.VMEM(nyquist.shape, jnp.bfloat16),
            pltpu.VMEM(fill.shape, f32),
            pltpu.VMEM(line.shape, f32),
            pltpu.VMEM(back.shape, jnp.bfloat16),
            pltpu.VMEM((rows * rows, half), f32),
            pltpu.VMEM((2, rows * rows, half), f32),
            pltpu.VMEM((planes + 1, rows, around), f32),
            pltpu.VMEM((3, planes, rows, around), f32),
            pltpu.VMEM((3, planes, rows, around), f32),
            pltpu.VMEM((planes, rows, around), f32),
            pltpu.VMEM((rows, around), f32),
            pltpu.VMEM((rows, around), f32),
            pltpu.VMEM((2, planes, rows, half), f32),
            pltpu.VMEM((planes, rows, half), f32),
            pltpu.VMEM((2, planes, rows, half), f32),
            pltpu.VMEM((owners, width, half), f32),
            pltpu.VMEM((gz_count, width, half), f32),
            pltpu.VMEM((gz_count, width, half), f32),
            pltpu.VMEM((2, owners, width, half), f32),
            pltpu.VMEM((planes + 1, rows, half), f32),
            pltpu.VMEM((planes + 1, rows, half), f32),
            pltpu.VMEM((planes + 1, rows, around), f32),
            dma((3,)),
            dma((13,)),
            dma((2,)),
            dma,
            dma((planes,)),
            dma((2,)),
            dma((2,)),
            dma,
            dma((owners,)),
            dma((2,)),
            pltpu.SemaphoreType.REGULAR(((gz_count // 2 - 1).bit_length(),)),
        ],
        compiler_params=pltpu.CompilerParams(
            collective_id=0, has_side_effects=True, vmem_limit_bytes=56 * 1024 * 1024
        ),
    )(
        offsets,
        diameters,
        phase_map,
        wall_mask,
        frac,
        velocity,
        gas_vel,
        jnp.asarray(ahead),
        jnp.asarray(nyquist),
        jnp.asarray(fill),
        jnp.asarray(line),
        jnp.asarray(back),
        jnp.asarray(first.reshape(rows * rows, half)),
    )
    return pl.pallas_call(
        put_kernel,
        out_shape=tuple(jax.ShapeDtypeStruct(x.shape, x.dtype) for x in results),
        in_specs=[pl.BlockSpec(memory_space=pltpu.VMEM)] * 2,
        out_specs=[pl.BlockSpec(memory_space=pl.ANY)] * 2,
        scratch_shapes=[dma((2,))],
        compiler_params=pltpu.CompilerParams(vmem_limit_bytes=4 * 1024 * 1024),
    )(*(pltpu.with_memory_space_constraint(x, pltpu.VMEM) for x in results))


def solution(mesh):
    in_specs = (
        P("ph", "gz", None, None),
        P("ph", None, "gz", None, None),
        P(None, "gz", None, None),
        P(),
        P("ph"),
        P(),
        P(),
    )
    out_specs = (P("gz", None, None), P("ph", None, "gz", None, None))
    gz_count, ph_count = mesh.shape["gz"], mesh.shape["ph"]

    def body(frac, *rest):
        rows, around = frac.shape[2:]
        fits = ph_count == 2 and around == 256 and rows <= 128 and gz_count % 4 == 0
        if fits and rows * 2 == gz_count * 8 and frac.shape[1] <= 8:
            return drum_step(gz_count, frac, *rest)
        return shards(frac, *rest)

    return jax.shard_map(body, mesh=mesh, in_specs=in_specs, out_specs=out_specs, check_vma=False)
```

```python
import functools
import math

import jax
import jax.numpy as jnp
import numpy as np
from jax import lax
from jax.experimental import pallas as pl
from jax.experimental.pallas import tpu as pltpu
from jax.sharding import PartitionSpec as P

DT_STEP = 0.5
DRAG_SCALE = 20.0
COMPRESS = 0.005
HIGHEST = lax.Precision.HIGHEST


def from_behind(block, axis, distance):
    devices = range(lax.axis_size(axis))
    route = [((i - distance) % len(devices), i) for i in devices]
    return lax.ppermute(block, axis, route)


def real_basis(count):
    index_rows = jnp.arange(count, dtype=jnp.int32)[:, None]
    column = jnp.arange(count, dtype=jnp.int32)[None, :]
    half = count // 2
    wave = jnp.where(column <= half, column, column - half)
    angle = 2.0 * math.pi / count * (index_rows * wave % count).astype(jnp.float32)
    scaled = math.sqrt(2.0 / count)
    cosine = jnp.cos(angle)
    table = jnp.where(column < half, scaled * cosine, scaled * jnp.sin(angle))
    return jnp.where((column == 0) | (column == half), cosine / math.sqrt(count), table)


def eigen_values(count):
    column = jnp.arange(count, dtype=jnp.int32)
    half = count // 2
    wave = jnp.where(column <= half, column, column - half).astype(jnp.float32)
    return 2.0 - 2.0 * jnp.cos(2.0 * math.pi / count * wave)


def rotate_mask(wall_mask, turns, around_count):
    around_idx = (
        jnp.arange(around_count, dtype=jnp.int32)[None, :] - turns[:, None]
    ) % around_count
    return jnp.transpose(jnp.take(wall_mask, around_idx, axis=1), (1, 0, 2)).astype(jnp.float32)


def radial_solve(spectral, axial_eig, theta_eig, radius_vec, angle_step):
    radial_count = radius_vec.shape[0]
    inner = radius_vec - 0.5
    outer = jnp.where(jnp.arange(radial_count) == radial_count - 1, 0.0, radius_vec + 0.5)
    diag = (
        COMPRESS
        + axial_eig[:, None, None]
        + theta_eig[None, :, None] / (radius_vec * angle_step) ** 2
        + ((outer + inner) / radius_vec)[None, None, :]
    )
    lower = jnp.broadcast_to(-inner / radius_vec, diag.shape)
    upper = jnp.broadcast_to(-outer / radius_vec, diag.shape)
    right = -jnp.transpose(spectral, (0, 2, 1))[..., None]
    solved = lax.linalg.tridiagonal_solve(lower, diag, upper, right)[..., 0]
    return jnp.transpose(solved, (0, 2, 1))


def to_space(modes, around_table):
    return jnp.dot(
        modes.reshape(-1, around_table.shape[0]), around_table.T, precision=HIGHEST
    ).reshape(modes.shape)


def shards(frac, velocity, gas_vel, diameters, phase_map, wall_mask, offsets):
    plane_count = frac.shape[1]
    radial_count = frac.shape[2]
    around_count = frac.shape[3]
    axial_total = offsets.shape[0]
    phase_count = lax.axis_size("ph")
    slab_index = lax.axis_index("gz")
    first_plane = slab_index * plane_count
    angle_step = 2.0 * math.pi / around_count
    plane_ids = (first_plane + jnp.arange(plane_count + 1, dtype=jnp.int32)) % axial_total
    fluid_all = rotate_mask(wall_mask, jnp.take(offsets, plane_ids), around_count)
    fluid = fluid_all[:plane_count]
    open_radial = fluid * jnp.concatenate([fluid[:, 1:], jnp.zeros_like(fluid[:, :1])], 1)
    open_around = fluid * jnp.roll(fluid, -1, 2)
    open_axial = fluid * fluid_all[1:]
    radius_vec = jnp.arange(radial_count, dtype=jnp.float32) + 0.5
    radii = radius_vec[:, None]
    which = (jnp.arange(diameters.shape[0], dtype=jnp.int32) == phase_map[0]).astype(jnp.float32)
    size_here = jnp.sum(diameters * which)
    volume = frac[0].astype(jnp.float32)
    gas = gas_vel.astype(jnp.float32)
    slip = velocity[0].astype(jnp.float32) - gas
    speed = jnp.sqrt(1.0 + jnp.sum(slip * slip, 0))
    beta = DRAG_SCALE * volume / (size_here * size_here) * (1.0 + 0.15 * speed)
    relax = 1.0 / (1.0 + DT_STEP * beta)
    predicted = gas + relax * slip
    share = volume * relax * slip + gas / phase_count
    flux_radial = share[0] * open_radial
    flux_around = share[1] * open_around
    flux_axial = share[2] * open_axial
    below = from_behind(flux_axial[-1:], "gz", 1)
    axial_prev = jnp.concatenate([below, flux_axial[:-1]], 0)
    radial_prev = jnp.concatenate([jnp.zeros_like(flux_radial[:, :1]), flux_radial[:, :-1]], 1)
    term = ((radii + 0.5) * flux_radial - (radii - 0.5) * radial_prev) / radii
    term = term + (flux_around - jnp.roll(flux_around, 1, 2)) / (radii * angle_step)
    term = (term + flux_axial - axial_prev) / DT_STEP
    around_table = real_basis(around_count)
    axial_table = real_basis(axial_total)
    axial_eig = eigen_values(axial_total)
    axial_step = None
    source = lax.psum(term, "ph")
    modes = jnp.dot(source.reshape(-1, around_count), around_table, precision=HIGHEST).reshape(
        source.shape
    )
    pencil = lax.all_to_all(modes, "gz", split_axis=2, concat_axis=0, tiled=True)
    mode_count = pencil.shape[2]
    theta_eig = lax.dynamic_slice_in_dim(
        eigen_values(around_count), slab_index * mode_count, mode_count
    )
    flat = pencil.reshape(axial_total, -1)
    spectral = jnp.dot(axial_table.T, flat, precision=HIGHEST).reshape(pencil.shape)
    solved = radial_solve(spectral, axial_eig, theta_eig, radius_vec, angle_step)
    space = jnp.dot(axial_table, solved.reshape(axial_total, -1), precision=HIGHEST).reshape(
        pencil.shape
    )
    ahead = jnp.roll(space, -1, 0) - space
    back, back_step = (
        lax.all_to_all(space, "gz", split_axis=0, concat_axis=2, tiled=True),
        lax.all_to_all(ahead, "gz", split_axis=0, concat_axis=2, tiled=True),
    )
    pressure = to_space(back, around_table)
    axial_step = to_space(back_step, around_table)
    radial_step = (jnp.concatenate([pressure[:, 1:], pressure[:, -1:]], 1) - pressure) * open_radial
    around_step = (jnp.roll(pressure, -1, 2) - pressure) / (radii * angle_step) * open_around
    gradient = jnp.stack([radial_step, around_step, axial_step * open_axial])
    corrected = (predicted - DT_STEP * gradient).astype(jnp.bfloat16)[None]
    return (pressure, corrected)


MESH_ID = pl.DeviceIdType.MESH


def split_low(x):
    high = x.astype(jnp.bfloat16)
    return high, (x - high.astype(jnp.float32)).astype(jnp.bfloat16)


def triple_dot(x, table_high, table_low):
    high, low = split_low(x)
    out = jnp.dot(high, table_high, preferred_element_type=jnp.float32)
    out = out + jnp.dot(low, table_high, preferred_element_type=jnp.float32)
    return out + jnp.dot(high, table_low, preferred_element_type=jnp.float32)


def np_high_low(table):
    high = table.astype(jnp.bfloat16)
    low = (table - high.astype(np.float64)).astype(jnp.bfloat16)
    return high, low


@functools.lru_cache(maxsize=None)
def operator_tables(radial, around, axial, planes):
    half = around // 2
    rows = np.arange(around)[:, None]
    column = np.arange(around)[None, :]
    wave = np.where(column <= half, column, column - half)
    angle = 2.0 * np.pi / around * (rows * wave % around)
    basis = np.sqrt(2.0 / around) * np.where(column <= half, np.cos(angle), np.sin(angle))
    basis = np.where((column == 0) | (column == half), np.cos(angle) / np.sqrt(around), basis)
    radius = np.arange(radial) + 0.5
    inner = radius - 0.5
    outer = np.where(np.arange(radial) == radial - 1, 0.0, radius + 0.5)
    step = 2.0 * np.pi / around
    vectors, values = [], []
    for m in range(half + 1):
        eig = 2.0 - 2.0 * np.cos(2.0 * np.pi / around * m)
        matrix = np.diag((outer + inner) / radius + eig / (radius * step) ** 2)
        off = -outer[:-1] / np.sqrt(radius[:-1] * radius[1:])
        matrix = matrix + np.diag(off, 1) + np.diag(off, -1)
        value, vector = np.linalg.eigh(matrix)
        vector = vector * np.where(vector[:1] < 0.0, -1.0, 1.0)
        values.append(value)
        vectors.append(vector)
    vectors = np.stack(vectors, -1)
    values = np.maximum(np.stack(values, -1), 0.0)
    first = vectors[:, :, :half]
    last = vectors[:, :, half]
    other = np.concatenate([values[:, half:], values[:, 1:half]], -1)
    over = COMPRESS + np.stack([values[:, :half], other])
    root = np.sqrt(over * (over + 4.0))
    ratio = 2.0 / (2.0 + over + root)
    jump = ratio**planes
    wrap = 1.0 / (1.0 - ratio**axial)
    line = np.stack([ratio, 1.0 / root, jump, wrap], 1).astype(np.float32)
    ahead = np_high_low(basis)
    back = np_high_low(basis.T.reshape(2, half, around))
    nyquist = np_high_low(last.T)
    fill = np.zeros((radial, max(radial, 128)))
    fill[:, :radial] = last / np.sqrt(radius)[:, None]
    return (
        first.astype(np.float32),
        np.stack(nyquist),
        fill.astype(np.float32),
        line,
        np.stack(ahead),
        np.stack(back),
    )


def left_triple(table_high, table_low, x):
    high, low = split_low(x)
    out = jnp.dot(table_high, high, preferred_element_type=jnp.float32)
    out = out + jnp.dot(table_high, low, preferred_element_type=jnp.float32)
    return out + jnp.dot(table_low, high, preferred_element_type=jnp.float32)


def drum_kernel(
    gz_count,
    offsets_hbm,
    diameters_hbm,
    map_hbm,
    wall_hbm,
    frac_hbm,
    velocity_hbm,
    gas_hbm,
    ahead_hbm,
    nyquist_hbm,
    fill_hbm,
    line_hbm,
    back_hbm,
    radial_hbm,
    pressure_ref,
    corrected_ref,
    offsets_ref,
    diameters_ref,
    map_ref,
    wall_ref,
    frac_ref,
    velocity_ref,
    gas_ref,
    ahead_ref,
    nyquist_ref,
    fill_ref,
    line_ref,
    back_ref,
    radial,
    radial_back,
    fluid,
    pred,
    gates,
    term,
    axial_flux,
    halo,
    modes,
    partner,
    lines,
    ends_out,
    ends_in,
    states_out,
    states_in,
    solved,
    result,
    result_other,
    space,
    scalar_sem,
    input_sem,
    halo_sem,
    swap_send,
    swap_recv,
    lines_sem,
    ends_sem,
    states_send,
    states_recv,
    relay_sem,
    known_sem,
):
    me = lax.axis_index("gz")
    ph = lax.axis_index("ph")
    other = 1 - ph
    planes, rows, around = term.shape
    half = around // 2
    axial_total = offsets_ref.shape[0]
    owners = gz_count // 2
    base = gz_count // 4
    width = ends_in.shape[1]
    blocks = owners // 2
    pair = blocks // 2
    half_rows = rows // 2
    angle_step = 2.0 * math.pi / around

    last = planes - 1
    streams = ((frac_hbm, frac_ref), (velocity_hbm, velocity_ref), (gas_hbm, gas_ref))

    def part(ref, start, count):
        lead = (slice(None),) * (len(ref.shape) - 3)
        return ref.at[(*lead, pl.ds(start, count))]

    tables = (
        (ahead_hbm, ahead_ref),
        (radial_hbm, radial),
        (nyquist_hbm, nyquist_ref),
        (fill_hbm, fill_ref),
        (line_hbm, line_ref),
        (back_hbm, back_ref),
    )
    pairs = [(part(a, last, 1), part(b, last, 1)) for a, b in streams]
    pairs += [(wall_hbm, wall_ref)]
    pairs += [(part(a, 0, last), part(b, 0, last)) for a, b in streams]
    pairs += tables
    fetches = [pltpu.make_async_copy(a, b, input_sem.at[i]) for i, (a, b) in enumerate(pairs)]
    small = ((offsets_hbm, offsets_ref), (diameters_hbm, diameters_ref), (map_hbm, map_ref))
    scalars = [pltpu.make_async_copy(a, b, scalar_sem.at[i]) for i, (a, b) in enumerate(small)]
    barrier = pltpu.get_barrier_semaphore()
    for fetch in scalars + fetches[:4]:
        fetch.start()
    for to in ((lax.rem(me + 1, gz_count), ph), (lax.rem(me + gz_count - 1, gz_count), ph)):
        pl.semaphore_signal(barrier, inc=1, device_id=to, device_id_type=MESH_ID)
    pl.semaphore_signal(barrier, inc=1, device_id=(me, other), device_id_type=MESH_ID)
    for fetch in fetches[4:8]:
        fetch.start()

    def greet(step):
        for to in (me + 2**step, me + gz_count - 2**step):
            pl.semaphore_signal(
                known_sem.at[step],
                inc=1,
                device_id=(lax.rem(to, gz_count), ph),
                device_id_type=MESH_ID,
            )

    steps = known_sem.shape[0]

    def spread(step):
        if step < steps:
            pl.semaphore_wait(known_sem.at[step], 2)
        if step + 1 < steps:
            greet(step + 1)

    radii = lax.broadcasted_iota(jnp.int32, (rows, around), 0).astype(jnp.float32) + 0.5
    row_id = lax.broadcasted_iota(jnp.int32, (rows, around), 0)
    lane = lax.broadcasted_iota(jnp.int32, (rows, half), 1)

    def rotate(z):
        turn = offsets_ref[lax.rem(me * planes + z, axial_total)]
        fluid[z] = pltpu.roll(wall_ref[...].astype(jnp.float32), turn, 1)

    for fetch in scalars + fetches[:4]:
        fetch.wait()
    rotate(planes)
    size = diameters_ref[map_ref[0]]

    arc = 1.0 / (radii * angle_step)

    def opens(z):
        rotate(z)
        here = fluid[z]
        open_radial = jnp.where(row_id == rows - 1, 0.0, here * pltpu.roll(here, rows - 1, 0))
        open_around = here * pltpu.roll(here, around - 1, 1)
        return open_radial, open_around, here * fluid[z + 1]

    weight = -jnp.sqrt(radii) / DT_STEP
    share = 1.0 / lax.axis_size("ph")

    def source(z):
        volume = frac_ref[0, z].astype(jnp.float32)
        gas = [gas_ref[a, z].astype(jnp.float32) for a in range(3)]
        slip = [velocity_ref[0, a, z].astype(jnp.float32) - gas[a] for a in range(3)]
        speed = jnp.sqrt(1.0 + (slip[0] * slip[0] + slip[1] * slip[1] + slip[2] * slip[2]))
        beta = DRAG_SCALE * volume / (size * size) * (1.0 + 0.15 * speed)
        relax = 1.0 / (1.0 + DT_STEP * beta)
        open_radial, open_around, open_axial = opens(z)
        for a in range(3):
            pred[a, z] = gas[a] + relax * slip[a]
        gates[0, z] = DT_STEP * open_radial
        gates[1, z] = (DT_STEP * arc) * open_around
        gates[2, z] = DT_STEP * open_axial
        pull = volume * relax
        flux_radial = (pull * slip[0] + share * gas[0]) * open_radial
        flux_around = (pull * slip[1] + share * gas[1]) * open_around
        flux_axial = (pull * slip[2] + share * gas[2]) * open_axial
        out = (radii + 0.5) * flux_radial
        inward = jnp.where(row_id == 0, 0.0, pltpu.roll(out, 1, 0))
        total = (out - inward) / radii
        total = total + (flux_around - pltpu.roll(flux_around, 1, 1)) * arc
        term[z] = (total + flux_axial) * weight
        return flux_axial

    def swap(z):
        return pltpu.make_async_remote_copy(
            src_ref=modes.at[other, z],
            dst_ref=partner.at[z],
            send_sem=swap_send,
            recv_sem=swap_recv.at[z],
            device_id=(me, other),
            device_id_type=MESH_ID,
        )

    def to_modes(z, behind):
        out = triple_dot(term[z] - behind * weight, ahead_ref[0], ahead_ref[1])
        modes[0, z] = out[:, :half]
        modes[1, z] = out[:, half:]
        swap(z).start()

    axial_flux[...] = source(last)
    for fetch in fetches[8:]:
        fetch.start()
    pl.semaphore_wait(barrier, 3)
    greet(0)
    halo_copy = pltpu.make_async_remote_copy(
        src_ref=axial_flux,
        dst_ref=halo,
        send_sem=halo_sem.at[0],
        recv_sem=halo_sem.at[1],
        device_id=(lax.rem(me + 1, gz_count), ph),
        device_id_type=MESH_ID,
    )
    halo_copy.start()
    for fetch in fetches[4:8]:
        fetch.wait()

    def send_modes(k, carry):
        z = planes - 2 - k
        to_modes(z + 1, source(z))
        return carry

    lax.fori_loop(0, planes - 1, send_modes, 0)
    halo_copy.wait()
    to_modes(0, halo[...])

    spread(0)
    for fetch in fetches[8:]:
        fetch.wait()

    def apply(table, loads, start=0, count=rows, accs=None):
        def add(k, accs):
            accs = list(accs)
            for j in range(8):
                r = start + k * 8 + j
                part = table[pl.ds(pl.multiple_of(r * rows, rows), rows), :]
                for i, load in enumerate(loads):
                    accs[i] = accs[i] + part * jnp.broadcast_to(load(r), (rows, half))
            return tuple(accs)

        if accs is None:
            accs = (jnp.zeros((rows, half), jnp.float32),) * len(loads)
        return lax.fori_loop(0, count // 8, add, tuple(accs))

    def forward(k, carry):
        z = planes - 1 - k
        swap(z).wait_recv()
        x = modes[ph, z] + partner[z]
        partner[z] = x
        (out,) = apply(radial, [lambda r: partner[z, pl.ds(r, 1), :]])
        exact = left_triple(nyquist_ref[0], nyquist_ref[1], x)
        lines[ph, z] = jnp.where(lane + other == 0, exact, out)
        return carry

    lax.fori_loop(0, planes // 2, forward, 0)
    spread(1)
    lax.fori_loop(planes // 2, planes, forward, 0)
    for step in range(2, steps):
        spread(step)

    ratio = line_ref[ph, 0]
    rising = lines[ph, 0]
    for z in range(1, planes):
        rising = rising * ratio + lines[ph, z]
    falling = lines[ph, planes - 1]
    for z in range(planes - 2, -1, -1):
        falling = falling * ratio + lines[ph, z]
    for j in range(blocks):
        o = j // pair * blocks + j % pair
        ends_out[o] = rising[width * j : width * j + width]
        ends_out[o + pair] = falling[width * j : width * j + width]

    is_owner = (me >= base) & (me < base + owners)

    def give_ends(o):
        return pltpu.make_async_remote_copy(
            src_ref=ends_out.at[o],
            dst_ref=ends_in.at[me],
            send_sem=ends_sem.at[0],
            recv_sem=ends_sem.at[1],
            device_id=(base + o, ph),
            device_id_type=MESH_ID,
        )

    def give_states(to, o):
        return pltpu.make_async_remote_copy(
            src_ref=states_out.at[to],
            dst_ref=states_in.at[ph, o],
            send_sem=states_send,
            recv_sem=states_recv.at[o],
            device_id=(to, ph),
            device_id_type=MESH_ID,
        )

    def relay(at, h):
        return pltpu.make_async_remote_copy(
            src_ref=states_in.at[h, at],
            dst_ref=states_in.at[h, at],
            send_sem=relay_sem.at[0],
            recv_sem=relay_sem.at[1 + at // blocks],
            device_id=(me, other),
            device_id_type=MESH_ID,
        )

    def whole(ref, send, recv):
        return pltpu.make_async_remote_copy(
            src_ref=ref,
            dst_ref=ref,
            send_sem=send,
            recv_sem=recv,
            device_id=(me, other),
            device_id_type=MESH_ID,
        )

    sent_ends = whole(ends_in.at[pl.ds(0, gz_count - 1)], ends_sem.at[0], ends_sem.at[1])

    def relayed(side):
        part = states_in.at[other, pl.ds(side * blocks, blocks)]
        return whole(part, relay_sem.at[0], relay_sem.at[1 + side])

    late = me // (gz_count // 2)

    for k in range(owners):
        side = 1 - late if k < blocks else late
        o = side * blocks + lax.rem(k + me, blocks)

        @pl.when(base + o != me)
        def _(o=o):
            give_ends(o).start()

    share_lines = whole(lines.at[ph], lines_sem.at[0], lines_sem.at[1])
    share_lines.start()

    @pl.when(is_owner)
    def _():
        ends_in[me] = ends_out[me - base]

    shrink = 1.0 / jnp.sqrt(radii[:, :half])

    def flip(l, carry):
        at = pl.ds(pl.multiple_of(l * rows, rows), rows)
        radial_back[0, at, :] = radial[pl.ds(l, rows, stride=rows), :] * shrink
        return carry

    lax.fori_loop(0, rows, flip, 0)

    @pl.when(is_owner)
    def _():
        sent_ends.wait_recv()
        mine = me - base
        is_rise = 1 - lax.rem(mine, blocks) // pair
        block = mine // blocks * pair + lax.rem(mine, pair)
        at = pl.ds(pl.multiple_of(block * width, width), width)
        jump = line_ref[ph, 2, at, :]
        wrap = line_ref[ph, 3, at, :]
        order = [is_rise * s + (1 - is_rise) * (gz_count - 1 - s) for s in range(gz_count)]
        state = jnp.zeros((width, half), jnp.float32)
        for s in range(gz_count):
            state = state * jump + ends_in[order[s]]
        state = state * wrap
        for s in range(gz_count):
            states_out[order[s]] = state
            state = state * jump + ends_in[order[s]]
        for hop in sorted(range(1, gz_count), key=lambda hop: abs(hop - gz_count // 2)):
            give_states(lax.rem(me + hop, gz_count), mine).start()
        states_in[ph, mine] = states_out[me]

    for l in range(rows):
        at = pl.ds(l * rows, rows)
        fill = jnp.broadcast_to(fill_ref[:, l : l + 1], (rows, half))
        radial_back[1, at, :] = jnp.where(lane == 0, fill, radial_back[0, at, :])

    def collect(side):
        for k in range(blocks):
            o = side * blocks + k

            @pl.when(base + o != me)
            def _(o=o):
                give_states(me, o).wait_recv()

            relay(o, ph).start()

    def solve(h, side):
        at = pl.ds(pl.multiple_of(side * half_rows, 8), half_rows)
        ratio = line_ref[h, 0, at, :]
        scale = line_ref[h, 1, at, :]
        states = [states_in[h, side * blocks + k] for k in range(blocks)]
        left = jnp.concatenate(states[:pair], 0)
        right = jnp.concatenate(states[pair:], 0)
        behind = right * ratio
        back = [None] * planes
        for z in range(planes - 1, -1, -1):
            back[z] = behind
            behind = (behind + lines[h, z, at, :]) * ratio
        for z in range(planes):
            left = left * ratio + lines[h, z, at, :]
            solved[z, at, :] = (back[z] + left) * scale
        solved[planes, at, :] = (right + left * ratio) * scale

    left_over = list(range(planes + 1))
    groups = []
    while left_over:
        groups.append(left_over[-4:])
        left_over = left_over[:-4]

    def inverse(h, at, side, accs):
        loads = [lambda r, z=z: solved[z, pl.ds(r, 1), :] for z in at]
        return apply(radial_back.at[h], loads, side * half_rows, half_rows, accs)

    def near_half(h, to):
        solve(h, late)
        for at in groups:
            for z, out in zip(at, inverse(h, at, late, None)):
                to[z] = out

    collect(late)
    near_half(ph, result)
    collect(1 - late)
    solve(ph, 1 - late)
    for at in groups:
        for z, out in zip(at, inverse(ph, at, 1 - late, [result[z] for z in at])):
            result[z] = out

    share_lines.wait_recv()
    relayed(late).wait_recv()
    near_half(other, result_other)
    relayed(1 - late).wait_recv()
    solve(other, 1 - late)

    def correct(z):
        here = space[z]
        pressure_ref[z] = here
        radial_step = (pltpu.roll(here, rows - 1, 0) - here) * gates[0, z]
        around_step = (pltpu.roll(here, around - 1, 1) - here) * gates[1, z]
        axial_step = (space[z + 1] - here) * gates[2, z]
        for a, step in enumerate((radial_step, around_step, axial_step)):
            corrected_ref[0, a, z] = (pred[a, z] - step).astype(jnp.bfloat16)

    before = []
    for at in groups:
        outs = inverse(other, at, 1 - late, [result_other[z] for z in at])
        own = jnp.concatenate([result[z] for z in at], 0)
        both = jnp.concatenate([own, jnp.concatenate(outs, 0)], 1)
        table = [jnp.concatenate([back_ref[i, ph], back_ref[i, other]], 0) for i in range(2)]
        found = triple_dot(both, *table)
        for z in before:
            correct(z)
        for i, z in enumerate(at):
            space[z] = found[i * rows : (i + 1) * rows]
        before = [z for z in at if z < planes]
    for z in before:
        correct(z)

    whole(modes.at[other], swap_send, swap_recv.at[0]).wait_send()
    share_lines.wait_send()
    whole(states_in.at[other], relay_sem.at[0], relay_sem.at[1]).wait_send()

    @pl.when(is_owner)
    def _():
        whole(ends_out.at[pl.ds(0, owners - 1)], ends_sem.at[0], ends_sem.at[1]).wait_send()
        sent = states_out.at[pl.ds(0, gz_count - 1)]
        whole(sent, states_send, states_recv.at[0]).wait_send()

    @pl.when(jnp.logical_not(is_owner))
    def _():
        whole(ends_out, ends_sem.at[0], ends_sem.at[1]).wait_send()


def put_kernel(pressure_vmem, corrected_vmem, pressure_out, corrected_out, sem):
    planes = pressure_vmem.shape[0]
    for z in range(planes):
        pltpu.make_async_copy(pressure_vmem.at[z], pressure_out.at[z], sem.at[0]).start()
        at = (0, slice(None), z)
        pltpu.make_async_copy(corrected_vmem.at[at], corrected_out.at[at], sem.at[1]).start()
    pltpu.make_async_copy(pressure_vmem, pressure_out, sem.at[0]).wait()
    pltpu.make_async_copy(corrected_vmem, corrected_out, sem.at[1]).wait()


def drum_step(gz_count, frac, velocity, gas_vel, diameters, phase_map, wall_mask, offsets):
    planes, rows, around = frac.shape[1:]
    half = around // 2
    first, nyquist, fill, line, ahead, back = operator_tables(rows, around, offsets.shape[0], planes)
    f32 = jnp.float32
    dma = pltpu.SemaphoreType.DMA
    owners = gz_count // 2
    width = 2 * rows // owners
    results = pl.pallas_call(
        functools.partial(drum_kernel, gz_count),
        out_shape=(
            pltpu.VMEM((planes, rows, around), f32),
            pltpu.VMEM((1, 3, planes, rows, around), jnp.bfloat16),
        ),
        in_specs=[pl.BlockSpec(memory_space=pl.ANY)] * 13,
        out_specs=[pl.BlockSpec(memory_space=pltpu.VMEM)] * 2,
        scratch_shapes=[
            pltpu.SMEM(offsets.shape, jnp.int32),
            pltpu.SMEM(diameters.shape, f32),
            pltpu.SMEM(phase_map.shape, jnp.int32),
            pltpu.VMEM(wall_mask.shape, jnp.int32),
            pltpu.VMEM(frac.shape, jnp.bfloat16),
            pltpu.VMEM(velocity.shape, jnp.bfloat16),
            pltpu.VMEM(gas_vel.shape, jnp.bfloat16),
            pltpu.VMEM(ahead.shape, jnp.bfloat16),
            pltpu.VMEM(nyquist.shape, jnp.bfloat16),
            pltpu.VMEM(fill.shape, f32),
            pltpu.VMEM(line.shape, f32),
            pltpu.VMEM(back.shape, jnp.bfloat16),
            pltpu.VMEM((rows * rows, half), f32),
            pltpu.VMEM((2, rows * rows, half), f32),
            pltpu.VMEM((planes + 1, rows, around), f32),
            pltpu.VMEM((3, planes, rows, around), f32),
            pltpu.VMEM((3, planes, rows, around), f32),
            pltpu.VMEM((planes, rows, around), f32),
            pltpu.VMEM((rows, around), f32),
            pltpu.VMEM((rows, around), f32),
            pltpu.VMEM((2, planes, rows, half), f32),
            pltpu.VMEM((planes, rows, half), f32),
            pltpu.VMEM((2, planes, rows, half), f32),
            pltpu.VMEM((owners, width, half), f32),
            pltpu.VMEM((gz_count, width, half), f32),
            pltpu.VMEM((gz_count, width, half), f32),
            pltpu.VMEM((2, owners, width, half), f32),
            pltpu.VMEM((planes + 1, rows, half), f32),
            pltpu.VMEM((planes + 1, rows, half), f32),
            pltpu.VMEM((planes + 1, rows, half), f32),
            pltpu.VMEM((planes + 1, rows, around), f32),
            dma((3,)),
            dma((13,)),
            dma((2,)),
            dma,
            dma((planes,)),
            dma((2,)),
            dma((2,)),
            dma,
            dma((owners,)),
            dma((3,)),
            pltpu.SemaphoreType.REGULAR(((gz_count // 2 - 1).bit_length(),)),
        ],
        compiler_params=pltpu.CompilerParams(
            collective_id=0, has_side_effects=True, vmem_limit_bytes=56 * 1024 * 1024
        ),
    )(
        offsets,
        diameters,
        phase_map,
        wall_mask,
        frac,
        velocity,
        gas_vel,
        jnp.asarray(ahead),
        jnp.asarray(nyquist),
        jnp.asarray(fill),
        jnp.asarray(line),
        jnp.asarray(back),
        jnp.asarray(first.reshape(rows * rows, half)),
    )
    return pl.pallas_call(
        put_kernel,
        out_shape=tuple(jax.ShapeDtypeStruct(x.shape, x.dtype) for x in results),
        in_specs=[pl.BlockSpec(memory_space=pltpu.VMEM)] * 2,
        out_specs=[pl.BlockSpec(memory_space=pl.ANY)] * 2,
        scratch_shapes=[dma((2,))],
        compiler_params=pltpu.CompilerParams(vmem_limit_bytes=4 * 1024 * 1024),
    )(*(pltpu.with_memory_space_constraint(x, pltpu.VMEM) for x in results))


def solution(mesh):
    in_specs = (
        P("ph", "gz", None, None),
        P("ph", None, "gz", None, None),
        P(None, "gz", None, None),
        P(),
        P("ph"),
        P(),
        P(),
    )
    out_specs = (P("gz", None, None), P("ph", None, "gz", None, None))
    gz_count, ph_count = mesh.shape["gz"], mesh.shape["ph"]

    def body(frac, *rest):
        rows, around = frac.shape[2:]
        fits = ph_count == 2 and around == 256 and rows <= 128 and gz_count % 8 == 0
        if fits and rows * 2 == gz_count * 8 and frac.shape[1] <= 8:
            return drum_step(gz_count, frac, *rest)
        return shards(frac, *rest)

    return jax.shard_map(body, mesh=mesh, in_specs=in_specs, out_specs=out_specs, check_vma=False)
```
